32 devices in a mesh: row: 8 (over z, y), col: 4 (over x, core).
Axes of the slice: x: 2, y: 2, z: 4, core: 2. Of those that a mesh axis runs over, the one named last changes fastest.
Arguments:
- momentum: float32 [8192, 8192], P('row', 'col'), may hold values from -6 to 6
- gradient: bfloat16 [8192, 8192], P('row', 'col'), may hold values from -6 to 6
- weight: bfloat16 [8192, 8192], P('row', 'col'), may hold values from -6 to 6
- right_start: float32 [8192, 512], P('col', 'row'), may hold values from -0.0625 to 0.0625
Outputs:
- new_momentum: float32 [8192, 8192], P('row', 'col')
- new_weight: bfloat16 [8192, 8192], P('row', 'col')
- new_right: float32 [8192, 512], P('col', 'row')
The draws below stay inside these ranges and needn't reach their ends.
All inputs are finite; a program needn't handle non-finite values.
Results may differ from the reference program's by a relative error of at most 0.001.
Values sent between devices are 32-bit elements; how exact they have to be, the bound alone decides.
A program may use at most 128 MiB of HBM per device.

```python
import jax
import jax.numpy as jnp
from jax import lax

OUT_DIM = 8192
IN_DIM = 8192
RANK = 512
ITERS = 2


def levels(key, dims, shards, least, top_value):
    loudness = 1.0
    for axis_at, blocks in shards:
        steps = jax.random.uniform(jax.random.fold_in(jax.random.fold_in(key, 6), axis_at), (blocks,), jnp.float32, least / len(shards), top_value / len(shards))
        loudness = loudness * jnp.repeat(jnp.exp(steps), dims[axis_at] // blocks).reshape((-1,) + (1,) * (len(dims) - 1 - axis_at))
    return loudness


def noise(key, dims, spread, most, split=(), held_as=jnp.bfloat16):
    factor_of = levels(key, dims, split, -0.22, 0.18) if split else 1.0
    result = jax.random.normal(key, dims, jnp.float32) * spread * factor_of
    return jnp.minimum(jnp.maximum(result, -most), most).astype(held_as)


def setup_inputs(seed: int = 0) -> dict:
    arg_keys = jax.random.split(jax.random.key(seed), 5)
    return {
        "momentum": noise(arg_keys[0], (OUT_DIM, IN_DIM), 1.0, 6.0, ((0, 8), (1, 4)), jnp.float32),
        "gradient": noise(arg_keys[1], (OUT_DIM, IN_DIM), 1.0, 6.0, ((0, 8), (1, 4))),
        "weight": noise(arg_keys[2], (OUT_DIM, IN_DIM), 1.0, 6.0, ((0, 8), (1, 4))),
        "right_start": noise(arg_keys[3], (IN_DIM, RANK), IN_DIM ** -0.5, 0.0625, ((0, 4), (1, 8)), jnp.float32),
    }


precise_mode = lax.Precision.HIGHEST
momentum_decay = 0.9
step_rate = 0.1
epsilon = 1e-06

def orthonormal(partials):
    gram_sum = jnp.dot(partials.T, partials, precision=precise_mode)
    triangle = jnp.linalg.cholesky(gram_sum)
    return jax.scipy.linalg.solve_triangular(triangle, partials.T, lower=True).T

def reference(momentum, gradient, weight, right_start):
    blended = momentum + gradient.astype(jnp.float32)
    right_factor = right_start
    for iteration in range(ITERS):
        left_rows = orthonormal(jnp.dot(blended, right_factor, precision=precise_mode))
        products = jnp.dot(left_rows.T, blended, precision=precise_mode).T
        col_norms = jnp.sqrt(lax.optimization_barrier(jnp.sum(products * products, axis=0, keepdims=True)) + epsilon)
        right_factor = products / col_norms
    new_momentum = blended - (1.0 - momentum_decay) * jnp.dot(left_rows, products.T, precision=precise_mode)
    scale_factor = step_rate * (OUT_DIM * IN_DIM / RANK) ** 0.5
    update = jnp.dot(left_rows, right_factor.T, precision=precise_mode)
    new_weight = (weight.astype(jnp.float32) - scale_factor * update).astype(jnp.bfloat16)
    return (new_momentum, new_weight, right_factor)
```

```python
import functools

import jax
import jax.numpy as jnp
from jax import lax
from jax.experimental import pallas as pl
from jax.experimental.pallas import tpu as pltpu
from jax.sharding import PartitionSpec as P

ITERS = 2
CORES = 2
momentum_decay = 0.9
step_rate = 0.1
epsilon = 1e-06
exact = lax.Precision.HIGHEST
f32, bf16 = jnp.float32, jnp.bfloat16
VMEM = pl.BlockSpec(memory_space=pltpu.VMEM)
MESH = pl.DeviceIdType.MESH
LIMIT = 56 << 20


def nt(a, b, precision=None):
    return lax.dot_general(a, b, (((1,), (1,)), ((), ())), precision=precision, preferred_element_type=f32)


def nn(a, b, precision=None):
    return lax.dot_general(a, b, (((1,), (0,)), ((), ())), precision=precision, preferred_element_type=f32)


def split(x):
    high = x.astype(bf16)
    return high, (x - high.astype(f32)).astype(bf16)


def three(dot, a, b):
    return (dot(a[1], b[0]) + dot(a[0], b[1])) + dot(a[0], b[0])


def outer_factor(n):
    d = 1
    while d * d < n or n % d:
        d += 1
    return d


def cost(flops, moved):
    return pl.CostEstimate(flops=int(flops), bytes_accessed=int(moved), transcendentals=0)


def eye(n):
    return (lax.broadcasted_iota(jnp.int32, (n, n), 0) == lax.broadcasted_iota(jnp.int32, (n, n), 1)).astype(f32)


def eliminate(a, w):
    size = a.shape[0]
    shape = (8, size)
    sub = lax.broadcasted_iota(jnp.int32, shape, 0)
    w[...] = eye(size)
    for at in range(0, size, 8):
        slab, inv_rows = a[at : at + 8, :], w[at : at + 8, :]
        cols = [jnp.broadcast_to(slab[:, at + i : at + i + 1], shape) for i in range(8)]
        scale = jnp.zeros(shape, f32)
        for i in range(8):
            pivot = jnp.broadcast_to(cols[i][i : i + 1, :], shape)
            scale = jnp.where(sub == i, lax.rsqrt(pivot), scale)
            if i < 7:
                m = jnp.where(sub > i, cols[i] / pivot, 0.0)
                for k in range(i + 1, 8):
                    cols[k] = cols[k] - m * jnp.broadcast_to(cols[k][i : i + 1, :], shape)
                slab = slab - m * jnp.broadcast_to(slab[i : i + 1, :], shape)
                inv_rows = inv_rows - m * jnp.broadcast_to(inv_rows[i : i + 1, :], shape)
        upper, inv_rows = slab * scale, inv_rows * scale
        w[at : at + 8, :] = inv_rows
        lower = upper.T
        for k in range(at + 8, size, 8):
            rows, inv = a[k : k + 8, :], w[k : k + 8, :]
            for i in range(8):
                factor = jnp.broadcast_to(lower[k : k + 8, i : i + 1], shape)
                rows = rows - factor * jnp.broadcast_to(upper[i : i + 1, :], shape)
                inv = inv - factor * jnp.broadcast_to(inv_rows[i : i + 1, :], shape)
            a[k : k + 8, :] = rows
            w[k : k + 8, :] = inv


def factor_kernel(gram, x, work, a, w):
    rank, block = gram.shape[0], a.shape[0]
    work[...] = gram[...]
    x[...] = eye(rank)
    for at in range(0, rank, block):
        end = at + block
        a[...] = work[at:end, at:end]
        eliminate(a, w)
        inverse = w[...]
        x[at:end, :] = nn(inverse, x[at:end, :], exact)
        if end < rank:
            panel = nt(work[end:, at:end], inverse, exact)
            work[end:, end:] = work[end:, end:] - nt(panel, panel, exact)
            x[end:, :] = x[end:, :] - nn(panel, x[at:end, :], exact)


def inverse_factor(gram):
    rank = gram.shape[0]
    block = min(128, rank)
    return pl.pallas_call(
        factor_kernel,
        name="factor",
        out_shape=jax.ShapeDtypeStruct((rank, rank), f32),
        in_specs=[VMEM],
        out_specs=VMEM,
        scratch_shapes=[pltpu.VMEM((rank, rank), f32)] + [pltpu.VMEM((block, block), f32)] * 2,
        cost_estimate=cost(2e10, 2 << 20),
    )(gram)


def prep_kernel(m, g, high, low):
    high[...], low[...] = split(m[...] + g[...].astype(f32))


def prepare(momentum, gradient):
    rows, cols = momentum.shape
    tile = min(256, rows)
    spec = pl.BlockSpec((tile, cols), lambda i: (i, 0))
    shape = jax.ShapeDtypeStruct((rows, cols), bf16)
    return pl.pallas_call(
        prep_kernel,
        name="prepare",
        grid=(rows // tile,),
        in_specs=[spec, spec],
        out_specs=[spec, spec],
        out_shape=[shape, shape],
        cost_estimate=cost(2 * rows * cols, 10 * rows * cols),
    )(momentum, gradient)


def first_kernel(r, high, low, out):
    part = three(nt, split(r[...]), (high[...], low[...]))
    step = pl.program_id(0)

    @pl.when(step == 0)
    def _():
        out[...] = part

    @pl.when(step > 0)
    def _():
        out[...] = out[...] + part


def row_sums(total):
    rank = total.shape[0]
    column = jnp.sum(total, axis=1, keepdims=True)
    return jnp.broadcast_to(column, (rank, 128)).T[:8, :]


def solved_kernel(multiply, x, q, *refs):
    if multiply:
        high, low, solved, squares, out, total = refs
    else:
        solved, squares, total = refs
    s = three(nn, split(x[...]), split(q[...]))
    solved[...] = s
    sums = s[:, :128] * s[:, :128]
    for at in range(128, s.shape[1], 128):
        sums = sums + s[:, at : at + 128] * s[:, at : at + 128]
    step = pl.program_id(0)

    @pl.when(step == 0)
    def _():
        total[...] = sums

    @pl.when(step > 0)
    def _():
        total[...] = total[...] + sums

    if multiply:
        part = three(nt, split(s), (high[...], low[...]))

        @pl.when(step == 0)
        def _():
            out[...] = part

        @pl.when(step > 0)
        def _():
            out[...] = out[...] + part

    @pl.when(step == pl.num_programs(0) - 1)
    def _():
        squares[...] = row_sums(total[...])


def first_product(right, high, low):
    rank, (rows, cols) = right.shape[0], high.shape
    wide = min(512, cols)
    block = pl.BlockSpec((rows, wide), lambda j: (0, j))
    return pl.pallas_call(
        first_kernel,
        name="first",
        grid=(cols // wide,),
        in_specs=[pl.BlockSpec((rank, wide), lambda j: (0, j)), block, block],
        out_specs=pl.BlockSpec((rank, rows), lambda j: (0, 0)),
        out_shape=jax.ShapeDtypeStruct((rank, rows), f32),
        compiler_params=pltpu.CompilerParams(vmem_limit_bytes=LIMIT),
        cost_estimate=cost(6 * rank * rows * cols, 4 * rows * cols),
    )(right, high, low)


def solved_product(x, q, high=None, low=None):
    rank, cols = q.shape
    wide = min(512, cols)
    block = pl.BlockSpec((rank, wide), lambda j: (0, j))
    in_specs = [pl.BlockSpec((rank, rank), lambda j: (0, 0)), block]
    out_specs = [block, pl.BlockSpec((8, rank), lambda j: (0, 0))]
    out_shape = [jax.ShapeDtypeStruct((rank, cols), f32), jax.ShapeDtypeStruct((8, rank), f32)]
    args = [x, q]
    if high is not None:
        rows = high.shape[0]
        in_specs += [pl.BlockSpec((rows, wide), lambda j: (0, j))] * 2
        out_specs.append(pl.BlockSpec((rank, rows), lambda j: (0, 0)))
        out_shape.append(jax.ShapeDtypeStruct((rank, rows), f32))
        args += [high, low]
    return pl.pallas_call(
        functools.partial(solved_kernel, high is not None),
        name="solved",
        grid=(cols // wide,),
        in_specs=in_specs,
        out_specs=out_specs,
        out_shape=out_shape,
        scratch_shapes=[pltpu.VMEM((rank, 128), f32)],
        compiler_params=pltpu.CompilerParams(vmem_limit_bytes=LIMIT),
        cost_estimate=cost(12 * rank * rank * cols, 8 * rank * cols),
    )(*args)


def left_kernel(x, p, high, low):
    s = three(nn, split(x[...]), split(p[...])).T
    high[...], low[...] = split(s)


def left_factor(x, p):
    rank, rows = p.shape
    wide = min(256, rows)
    block = pl.BlockSpec((wide, rank), lambda j: (j, 0))
    shape = jax.ShapeDtypeStruct((rows, rank), bf16)
    return pl.pallas_call(
        left_kernel,
        name="left",
        grid=(rows // wide,),
        in_specs=[pl.BlockSpec((rank, rank), lambda j: (0, 0)), pl.BlockSpec((rank, wide), lambda j: (0, j))],
        out_specs=[block, block],
        out_shape=[shape, shape],
        compiler_params=pltpu.CompilerParams(vmem_limit_bytes=LIMIT),
        cost_estimate=cost(6 * rank * rank * rows, 8 * rank * rows),
    )(x, p)


def final_kernel(scale_factor, high, low, q, norms, m, g, weight, new_m, new_w):
    rank = q.shape[0]
    column = jnp.broadcast_to(norms[0:1, :], (128, rank)).T[:, 0:1]
    s = q[...]
    left = (high[...], low[...])
    blended = m[...] + g[...].astype(f32)
    new_m[...] = blended - (1.0 - momentum_decay) * nn(left[0], s.astype(bf16))
    update = three(nn, left, split(s / column))
    new_w[...] = (weight[...].astype(f32) - scale_factor * update).astype(bf16)


def outputs(scale_factor, high, low, q, norms, momentum, gradient, weight):
    rank, cols = q.shape
    rows = high.shape[0]
    wide = min(256, cols)
    side = pl.BlockSpec((rows, rank), lambda j: (0, 0))
    block = pl.BlockSpec((rows, wide), lambda j: (0, j))
    return pl.pallas_call(
        functools.partial(final_kernel, scale_factor),
        name="outputs",
        grid=(cols // wide,),
        in_specs=[side, side, pl.BlockSpec((rank, wide), lambda j: (0, j)), pl.BlockSpec((8, rank), lambda j: (0, 0)), block, block, block],
        out_specs=[block, block],
        out_shape=[jax.ShapeDtypeStruct((rows, cols), f32), jax.ShapeDtypeStruct((rows, cols), bf16)],
        compiler_params=pltpu.CompilerParams(vmem_limit_bytes=LIMIT),
        cost_estimate=cost(8 * rank * rows * cols, 14 * rows * cols),
    )(high, low, q, norms, momentum, gradient, weight)


class Place:
    def __init__(self, rows, cols):
        self.deep = outer_factor(rows)
        self.flat = rows // self.deep
        self.wide = cols // CORES
        self.row, self.col = lax.axis_index("row"), lax.axis_index("col")
        self.z, self.y = self.row // self.flat, self.row % self.flat
        self.x, self.core = self.col // CORES, self.col % CORES

    def to_y(self, d):
        return (self.z * self.flat + (self.y + d) % self.flat, self.col)

    def to_z(self, d):
        return (((self.z + d) % self.deep) * self.flat + self.y, self.col)

    def to_x(self, d):
        return (self.row, ((self.x + d) % self.wide) * CORES + self.core)

    def partner(self):
        return (self.row, self.x * CORES + 1 - self.core)

    def y_peers(self):
        return [self.to_y(d) for d in range(1, self.flat)]

    def z_peers(self):
        return [self.to_z(d) for d in range(1, self.deep)]

    def x_peers(self):
        return [self.to_x(d) for d in range(1, self.wide)]


def greet(peers):
    barrier = pltpu.get_barrier_semaphore()
    for peer in peers:
        pl.semaphore_signal(barrier, inc=1, device_id=peer, device_id_type=MESH)
    pl.semaphore_wait(barrier, len(peers))


class Sender:
    def __init__(self, send, recv):
        self.send, self.recv, self.copies = send, recv, []

    def start(self, src, dst, peer):
        at = len(self.copies)
        copy = pltpu.make_async_remote_copy(
            src_ref=src, dst_ref=dst, send_sem=self.send.at[at], recv_sem=self.recv.at[at], device_id=peer, device_id_type=MESH
        )
        copy.start()
        self.copies.append(copy)
        return copy

    def drain(self):
        for copy in self.copies:
            copy.wait_send()


def join_kernel(rows, cols, pieces, scaled, *refs):
    if scaled:
        p, sq, out, gram, norms, half, near, far, sq_in, send, recv = refs
    else:
        p, out, gram, half, near, far, send, recv = refs
    at = Place(rows, cols)
    greet([at.partner()] + at.x_peers() + ([(at.row, (at.x + d) % at.wide * CORES + 1 - at.core) for d in range(1, at.wide)] if scaled else []))
    go = Sender(send, recv)
    mine, other = at.core, 1 - at.core
    squares = []
    if scaled:
        for d in range(1, cols):
            squares.append(go.start(sq, sq_in.at[d - 1], (at.row, (at.col + d) % cols)))
    first = [go.start(p.at[other, k], near.at[k], at.partner()) for k in range(pieces)]
    second = []
    for k in range(pieces):
        first[k].wait_recv()
        half[k] = p[mine, k] + near[k]
        second.append([go.start(half.at[k], far.at[d, k], peer) for d, peer in enumerate(at.x_peers())])
    if scaled:
        total = sq[...]
        for d, copy in enumerate(squares):
            copy.wait_recv()
            total = total + sq_in[d]
        norm = jnp.sqrt(total + epsilon)
        norms[...] = norm
        rank = norm.shape[1]
        column = jnp.broadcast_to(norm[0:1, :], (128, rank)).T[:, 0:1]
        size = rank // (CORES * pieces)
        columns = [column[k * size : (k + 1) * size] for k in range(CORES * pieces)]
    third = []
    for k in range(pieces):
        total = half[k]
        for d, copy in enumerate(second[k]):
            copy.wait_recv()
            total = total + far[d, k]
        if scaled:
            total = total / jnp.where(mine == 0, columns[k], columns[pieces + k])
        out[mine, k] = total
        third.append(go.start(out.at[mine, k], out.at[mine, k], at.partner()))
    for copy in third:
        copy.wait_recv()
    full = out[...].reshape(-1, p.shape[-1])
    share = gram.shape[0]
    own = p.shape[2] // share if share < p.shape[2] else 1
    if share <= p.shape[2]:
        piece = at.col // own
        lines = out[piece // pieces, piece % pieces, pl.ds(pl.multiple_of((at.col % own) * share, share), share), :]
    else:
        span = share // p.shape[2]
        lines = out[at.col * span // pieces, pl.ds((at.col * span) % pieces, span)].reshape(share, p.shape[-1])
    gram[...] = nt(lines, full, exact)
    go.drain()


def join(part, squares, rows, cols, ident):
    rank, lines = part.shape
    pieces = 4
    size = rank // (CORES * pieces)
    scaled = squares is not None
    wide = cols // CORES
    sends = 2 * pieces + pieces * (wide - 1) + (cols - 1 if scaled else 0)
    out_shape = [jax.ShapeDtypeStruct((CORES, pieces, size, lines), f32), jax.ShapeDtypeStruct((rank // cols, rank), f32)]
    scratch = [pltpu.VMEM((pieces, size, lines), f32)] * 2 + [pltpu.VMEM((wide - 1, pieces, size, lines), f32)]
    args = [part.reshape(CORES, pieces, size, lines)]
    if scaled:
        out_shape.append(jax.ShapeDtypeStruct(squares.shape, f32))
        scratch.append(pltpu.VMEM((cols - 1,) + squares.shape, f32))
        args.append(squares)
    res = pl.pallas_call(
        functools.partial(join_kernel, rows, cols, pieces, scaled),
        name="join",
        out_shape=out_shape,
        in_specs=[VMEM] * len(args),
        out_specs=[VMEM] * len(out_shape),
        scratch_shapes=scratch + [pltpu.SemaphoreType.DMA((sends,))] * 2,
        compiler_params=pltpu.CompilerParams(collective_id=ident, has_side_effects=True, vmem_limit_bytes=LIMIT),
        cost_estimate=cost(6e9, 6 << 20),
    )(*args)
    return [res[0].reshape(rank, lines)] + list(res[1:])


def norm_kernel(rows, cols, sq, norms, sq_in, send, recv):
    at = Place(rows, cols)
    peers = [(at.row, (at.col + d) % cols) for d in range(1, cols)]
    greet(peers)
    go = Sender(send, recv)
    copies = [go.start(sq, sq_in.at[d], peer) for d, peer in enumerate(peers)]
    total = sq[...]
    for d, copy in enumerate(copies):
        copy.wait_recv()
        total = total + sq_in[d]
    norms[...] = jnp.sqrt(total + epsilon)
    go.drain()


def column_norms(squares, rows, cols, ident):
    return pl.pallas_call(
        functools.partial(norm_kernel, rows, cols),
        name="norms",
        out_shape=jax.ShapeDtypeStruct(squares.shape, f32),
        in_specs=[VMEM],
        out_specs=VMEM,
        scratch_shapes=[pltpu.VMEM((cols - 1,) + squares.shape, f32)] + [pltpu.SemaphoreType.DMA((cols - 1,))] * 2,
        compiler_params=pltpu.CompilerParams(collective_id=ident, has_side_effects=True),
        cost_estimate=cost(1e6, 1 << 20),
    )(squares)


def scatter_kernel(rows, cols, p, gram, high, low, own, gall, ph, pw, q, yr, h, zr, gq, gyr, gh, gzr, send, recv):
    at = Place(rows, cols)
    greet(at.y_peers() + at.z_peers() + at.x_peers() + [at.partner()])
    go = Sender(send, recv)
    blocks, wide = q.shape[0], q.shape[-1]
    rank = p.shape[0]
    size, share = q.shape[3], gq.shape[2]

    def start_y(src, into):
        return [go.start(src.at[:, (at.y + d) % at.flat], into.at[d - 1], at.to_y(d)) for d in range(1, at.flat)]

    def middle(src, into, copies, sums, zinto):
        total = src[:, pl.ds(at.y, 1)][:, 0]
        for d, copy in enumerate(copies):
            copy.wait_recv()
            total = total + into[d]
        sums[...] = total
        return [go.start(sums.at[(at.z + d) % at.deep], zinto.at[d - 1], at.to_z(d)) for d in range(1, at.deep)]

    def last(sums, zinto, copies):
        total = sums[pl.ds(at.z, 1)][0]
        for d, copy in enumerate(copies):
            copy.wait_recv()
            total = total + zinto[d]
        return total

    for i in range(at.deep):
        for j in range(at.flat):
            k = (i * at.flat + j) * share
            gq[i, j] = gram[k : k + share, :]
    gy = start_y(gq, gyr)
    ph[...], pw[...] = split(p[...])
    line = 256

    def multiply(j):
        columns = slice(j * wide, (j + 1) * wide)

        def some(i, carry):
            span = pl.ds(pl.multiple_of(i * line, line), line)
            value = three(nn, (ph[span, :], pw[span, :]), (high[:, columns], low[:, columns]))
            for k in range(line // size):
                chunk = i * (line // size) + k
                q[j, chunk // at.flat, chunk % at.flat] = value[k * size : (k + 1) * size, :]
            return carry

        lax.fori_loop(0, rank // line, some, 0)

    ys, zs = [], []
    gz = gz2 = gy2 = gx = None
    for j in range(blocks):
        multiply(j)
        ys.append(start_y(q.at[j], yr.at[j]))
        if j == 0:
            gz = middle(gq, gyr, gy, gh, gzr)
        if j == 1:
            mine = (at.x, at.core, at.z, at.y)
            gall[mine] = last(gh, gzr, gz)
            gz2 = [go.start(gall.at[mine], gall.at[mine], peer) for peer in at.z_peers()]
    for copy in gz2:
        copy.wait_recv()
    line_at = (at.x, at.core, slice(None), at.y)
    gy2 = [go.start(gall.at[line_at], gall.at[line_at], peer) for peer in at.y_peers()]
    for j in range(blocks):
        zs.append(middle(q.at[j], yr.at[j], ys[j], h.at[j], zr.at[j]))
    for copy in gy2:
        copy.wait_recv()
    gx = [go.start(gall.at[at.x, at.core], gall.at[at.x, at.core], peer) for peer in at.x_peers()]
    for j in range(blocks):
        own[:, j * wide : (j + 1) * wide] = last(h.at[j], zr.at[j], zs[j])
        if j == blocks // 2:
            for copy in gx:
                copy.wait_recv()
            gc = go.start(gall.at[:, at.core], gall.at[:, at.core], at.partner())
    gc.wait_recv()
    go.drain()


def scatter(p, gram, high, low, rows, cols, ident):
    rank, lines = p.shape
    width = high.shape[1]
    blocks = max(1, min(4, width // 256))
    deep = outer_factor(rows)
    flat = rows // deep
    wide, size, share = width // blocks, rank // rows, gram.shape[0] // rows
    xs = cols // CORES
    sends = (blocks + 1) * (deep + flat - 2) + (deep - 1) + (flat - 1) + (xs - 1) + 1
    own, gall = pl.pallas_call(
        functools.partial(scatter_kernel, rows, cols),
        name="scatter",
        out_shape=[jax.ShapeDtypeStruct((size, width), f32), jax.ShapeDtypeStruct((xs, CORES, deep, flat, share, rank), f32)],
        in_specs=[VMEM] * 4,
        out_specs=[VMEM] * 2,
        scratch_shapes=[
            pltpu.VMEM((rank, lines), bf16),
            pltpu.VMEM((rank, lines), bf16),
            pltpu.VMEM((blocks, deep, flat, size, wide), f32),
            pltpu.VMEM((blocks, flat - 1, deep, size, wide), f32),
            pltpu.VMEM((blocks, deep, size, wide), f32),
            pltpu.VMEM((blocks, deep - 1, size, wide), f32),
            pltpu.VMEM((deep, flat, share, rank), f32),
            pltpu.VMEM((flat - 1, deep, share, rank), f32),
            pltpu.VMEM((deep, share, rank), f32),
            pltpu.VMEM((deep - 1, share, rank), f32),
            pltpu.SemaphoreType.DMA((sends,)),
            pltpu.SemaphoreType.DMA((sends,)),
        ],
        compiler_params=pltpu.CompilerParams(collective_id=ident, has_side_effects=True, vmem_limit_bytes=LIMIT),
        cost_estimate=cost(6 * rank * lines * width, 4 * lines * width),
    )(p, gram, high, low)
    return own, gall.reshape(rank, rank)


def shards(rows, cols, momentum, gradient, weight, right_start):
    out_dim, in_dim = momentum.shape[0] * rows, momentum.shape[1] * cols
    rank = right_start.shape[1] * rows
    right = lax.all_gather(right_start.T, "row", axis=0, tiled=True)
    high, low = prepare(momentum, gradient)
    partials, squares = first_product(right, high, low), None
    for iteration in range(ITERS):
        joined = join(partials, squares, rows, cols, 2 * iteration)
        own, gram = scatter(joined[0], joined[1], high, low, rows, cols, 9)
        x = inverse_factor(gram)
        whole = lax.all_gather(own, "row", axis=0, tiled=True)
        if iteration + 1 < ITERS:
            products, squares, partials = solved_product(x, whole, high, low)
    left_high, left_low = left_factor(x, joined[0])
    products, squares = solved_product(x, whole)
    norms = column_norms(squares, rows, cols, 8)
    scale_factor = step_rate * (out_dim * in_dim / rank) ** 0.5
    new_momentum, new_weight = outputs(scale_factor, left_high, left_low, products, norms, momentum, gradient, weight)
    size = rank // rows
    start = lax.axis_index("row") * size
    some = lax.dynamic_slice_in_dim(products, start, size, axis=0)
    norm = lax.dynamic_slice_in_dim(norms[0], start, size, axis=0)
    return new_momentum, new_weight, (some / norm[:, None]).T


def solution(mesh):
    rows, cols = mesh.shape["row"], mesh.shape["col"]
    return jax.shard_map(
        functools.partial(shards, rows, cols),
        mesh=mesh,
        in_specs=(P("row", "col"), P("row", "col"), P("row", "col"), P("col", "row")),
        out_specs=(P("row", "col"), P("row", "col"), P("col", "row")),
        check_vma=False,
    )
```

```python
import functools

import jax
import jax.numpy as jnp
from jax import lax
from jax.experimental import pallas as pl
from jax.experimental.pallas import tpu as pltpu
from jax.sharding import PartitionSpec as P

ITERS = 2
CORES = 2
momentum_decay = 0.9
step_rate = 0.1
epsilon = 1e-06
exact = lax.Precision.HIGHEST
f32, bf16 = jnp.float32, jnp.bfloat16
VMEM = pl.BlockSpec(memory_space=pltpu.VMEM)
MESH = pl.DeviceIdType.MESH
LIMIT = 56 << 20


def nt(a, b, precision=None):
    return lax.dot_general(a, b, (((1,), (1,)), ((), ())), precision=precision, preferred_element_type=f32)


def nn(a, b, precision=None):
    return lax.dot_general(a, b, (((1,), (0,)), ((), ())), precision=precision, preferred_element_type=f32)


def split(x):
    high = x.astype(bf16)
    return high, (x - high.astype(f32)).astype(bf16)


def three(dot, a, b):
    return (dot(a[1], b[0]) + dot(a[0], b[1])) + dot(a[0], b[0])


def outer_factor(n):
    d = 1
    while d * d < n or n % d:
        d += 1
    return d


def cost(flops, moved):
    return pl.CostEstimate(flops=int(flops), bytes_accessed=int(moved), transcendentals=0)


def eye(n):
    return (lax.broadcasted_iota(jnp.int32, (n, n), 0) == lax.broadcasted_iota(jnp.int32, (n, n), 1)).astype(f32)


def eliminate(a, w):
    size = a.shape[0]
    shape = (8, size)
    sub = lax.broadcasted_iota(jnp.int32, shape, 0)
    w[...] = eye(size)
    for at in range(0, size, 8):
        slab, inv_rows = a[at : at + 8, :], w[at : at + 8, :]
        cols = [jnp.broadcast_to(slab[:, at + i : at + i + 1], shape) for i in range(8)]
        scale = jnp.zeros(shape, f32)
        for i in range(8):
            pivot = jnp.broadcast_to(cols[i][i : i + 1, :], shape)
            scale = jnp.where(sub == i, lax.rsqrt(pivot), scale)
            if i < 7:
                m = jnp.where(sub > i, cols[i] / pivot, 0.0)
                for k in range(i + 1, 8):
                    cols[k] = cols[k] - m * jnp.broadcast_to(cols[k][i : i + 1, :], shape)
                slab = slab - m * jnp.broadcast_to(slab[i : i + 1, :], shape)
                inv_rows = inv_rows - m * jnp.broadcast_to(inv_rows[i : i + 1, :], shape)
        upper, inv_rows = slab * scale, inv_rows * scale
        w[at : at + 8, :] = inv_rows
        lower = upper.T
        for k in range(at + 8, size, 8):
            rows, inv = a[k : k + 8, :], w[k : k + 8, :]
            for i in range(8):
                factor = jnp.broadcast_to(lower[k : k + 8, i : i + 1], shape)
                rows = rows - factor * jnp.broadcast_to(upper[i : i + 1, :], shape)
                inv = inv - factor * jnp.broadcast_to(inv_rows[i : i + 1, :], shape)
            a[k : k + 8, :] = rows
            w[k : k + 8, :] = inv


def factor_step(step, work, x, a, w):
    rank, block = work.shape[0], a.shape[0]
    span = pl.ds(pl.multiple_of(step * block, block), block)
    a[...] = work[span, span]
    eliminate(a, w)
    inverse = w[...]
    below = lax.broadcasted_iota(jnp.int32, (rank, block), 0) >= (step + 1) * block
    panel = jnp.where(below, nt(work[:, span], inverse, exact), 0.0)
    solved = nn(inverse, x[span, :], exact)
    x[...] = x[...] - nn(panel, solved, exact)
    x[span, :] = solved
    work[...] = work[...] - nt(panel, panel, exact)


def row_sums(total):
    rank = total.shape[0]
    column = jnp.sum(total, axis=1, keepdims=True)
    return jnp.broadcast_to(column, (rank, 128)).T[:8, :]


def final_kernel(scale_factor, high, low, q, norms, m, g, weight, new_m, new_w):
    rank = q.shape[0]
    column = jnp.broadcast_to(norms[0:1, :], (128, rank)).T[:, 0:1]
    s = q[...]
    left = (high[...], low[...])
    blended = m[...] + g[...].astype(f32)
    new_m[...] = blended - (1.0 - momentum_decay) * nn(left[0], s.astype(bf16))
    update = three(nn, left, split(s / column))
    new_w[...] = (weight[...].astype(f32) - scale_factor * update).astype(bf16)


def outputs(scale_factor, high, low, q, norms, momentum, gradient, weight):
    rank, cols = q.shape
    rows = high.shape[0]
    wide = min(256, cols)
    side = pl.BlockSpec((rows, rank), lambda j: (0, 0))
    block = pl.BlockSpec((rows, wide), lambda j: (0, j))
    return pl.pallas_call(
        functools.partial(final_kernel, scale_factor),
        name="outputs",
        grid=(cols // wide,),
        in_specs=[side, side, pl.BlockSpec((rank, wide), lambda j: (0, j)), pl.BlockSpec((8, rank), lambda j: (0, 0)), block, block, block],
        out_specs=[block, block],
        out_shape=[jax.ShapeDtypeStruct((rows, cols), f32), jax.ShapeDtypeStruct((rows, cols), bf16)],
        compiler_params=pltpu.CompilerParams(vmem_limit_bytes=LIMIT),
        cost_estimate=cost(8 * rank * rows * cols, 14 * rows * cols),
    )(high, low, q, norms, momentum, gradient, weight)


class Place:
    def __init__(self, rows, cols):
        self.deep = outer_factor(rows)
        self.flat = rows // self.deep
        self.wide = cols // CORES
        self.row, self.col = lax.axis_index("row"), lax.axis_index("col")
        self.z, self.y = self.row // self.flat, self.row % self.flat
        self.x, self.core = self.col // CORES, self.col % CORES

    def to_y(self, d):
        return (self.z * self.flat + (self.y + d) % self.flat, self.col)

    def to_z(self, d):
        return (((self.z + d) % self.deep) * self.flat + self.y, self.col)

    def to_x(self, d):
        return (self.row, ((self.x + d) % self.wide) * CORES + self.core)

    def partner(self):
        return (self.row, self.x * CORES + 1 - self.core)

    def y_peers(self):
        return [self.to_y(d) for d in range(1, self.flat)]

    def z_peers(self):
        return [self.to_z(d) for d in range(1, self.deep)]

    def x_peers(self):
        return [self.to_x(d) for d in range(1, self.wide)]


def greet(peers):
    barrier = pltpu.get_barrier_semaphore()
    for peer in peers:
        pl.semaphore_signal(barrier, inc=1, device_id=peer, device_id_type=MESH)
    pl.semaphore_wait(barrier, len(peers))


class Sender:
    def __init__(self, send, recv):
        self.send, self.recv, self.copies = send, recv, []

    def start(self, src, dst, peer):
        at = len(self.copies)
        copy = pltpu.make_async_remote_copy(
            src_ref=src, dst_ref=dst, send_sem=self.send.at[at], recv_sem=self.recv.at[at], device_id=peer, device_id_type=MESH
        )
        copy.start()
        self.copies.append(copy)
        return copy

    def drain(self):
        for copy in self.copies:
            copy.wait_send()


PIECES = 4


def iterate_kernel(rows, cols, units, blocks, mode, *refs):
    if mode == 0:
        own, m, g, high, low, out, chunk, gall = refs[:8]
        refs = refs[8:]
    else:
        own, gram, high, low, out, chunk, gall = refs[:7]
        x, xh, xl, a, w, work, total, sq, sq_in, ss, sr = refs[7:18]
        refs = refs[18:]
    whole, part, half, near, far, gram_own, ph, pw, q, qy, h, hz, gq, gyr, gh, gzr, zs, zr, ys, yr = refs[:20]
    join_s, join_r, far_s, far_r, back_s, back_r, qy_s, qy_r, hz_s, hz_r, send, recv = refs[20:]
    at = Place(rows, cols)
    peers = at.y_peers() + at.z_peers()
    col_peers = [(at.row, (at.col + d) % cols) for d in range(1, cols)]
    greet(peers + (col_peers if mode else at.x_peers() + [at.partner()]))
    size, wide = whole.shape[3], whole.shape[4]
    rank, middle_rank = size * rows * (2 if mode else 1), part.shape[1] * part.shape[2] * part.shape[3]
    lines = part.shape[-1]
    step_lanes = units // 2

    def remote(src, dst, send_sem, recv_sem, peer):
        return pltpu.make_async_remote_copy(
            src_ref=src, dst_ref=dst, send_sem=send_sem, recv_sem=recv_sem, device_id=peer, device_id_type=MESH
        )

    def spread(at_index, count):
        if isinstance(at_index, int):
            return slice(at_index * count, (at_index + 1) * count)
        return pl.ds(pl.multiple_of(at_index * count, count), count)

    def loop(start, count, body):
        lax.fori_loop(start, count, lambda j, c: (body(j), c)[1], 0)

    def lanes(u):
        return spread(u % step_lanes, wide) if mode else spread(u, wide)

    def source(u):
        return own.at[u // step_lanes, :, lanes(u)] if mode else own.at[:, lanes(u)]

    def z_copy(u, d):
        return remote(source(u), whole.at[u, at.z, at.y], zs.at[u, d - 1], zr.at[u, d - 1], at.to_z(d))

    def y_copy(u, e, d):
        piece = whole.at[u, (at.z - d + at.deep) % at.deep, at.y]
        return remote(source(u) if d == 0 else piece, piece, ys.at[u, e - 1, d], yr.at[u, e - 1, d], at.to_y(e))

    for u in range(units):
        for d in range(1, at.deep):
            z_copy(u, d).start()
        for e in range(1, at.flat):
            y_copy(u, e, 0).start()
    for u in range(units):
        whole[u, at.z, at.y] = own[u // step_lanes, :, lanes(u)] if mode else own[:, lanes(u)]

    def forward(u):
        for d in range(1, at.deep):
            z_copy(u, d).wait_recv()
            for e in range(1, at.flat):
                y_copy(u, e, d).start()

    def arrived(u):
        for e in range(1, at.flat):
            for d in range(at.deep):
                y_copy(u, e, d).wait_recv()

    mine, other = at.core, 1 - at.core

    def near_copy(r, k):
        return remote(part.at[r, other, k], near.at[r, k], join_s.at[r, k], join_r.at[r, k], at.partner())

    def far_copy(r, k, d):
        return remote(half.at[r, k], far.at[r, d - 1, k], far_s.at[r, k, d - 1], far_r.at[r, k, d - 1], at.to_x(d))

    def back_copy(r, k):
        return remote(out.at[r, mine, k], out.at[r, mine, k], back_s.at[r, k], back_r.at[r, k], at.partner())

    def sq_copy(r, d):
        return remote(sq.at[r], sq_in.at[r, d - 1], ss.at[r, d - 1], sr.at[r, d - 1], (at.row, (at.col + d) % cols))

    def join_begin(r):
        if mode:
            sq[r] = row_sums(total[r])
            for d in range(1, cols):
                sq_copy(r, d).start()
        for k in range(PIECES):
            near_copy(r, k).start()
        for k in range(PIECES):
            near_copy(r, k).wait_recv()
            half[r, k] = part[r, mine, k] + near[r, k]
            for d in range(1, at.wide):
                far_copy(r, k, d).start()

    def join_end(r):
        if mode:
            value = sq[r]
            for d in range(1, cols):
                sq_copy(r, d).wait_recv()
                value = value + sq_in[r, d - 1]
            norm = jnp.sqrt(value + epsilon)
            column = jnp.broadcast_to(norm[0:1, :], (128, middle_rank)).T[:, 0:1]
            count = middle_rank // (CORES * PIECES)
        for k in range(PIECES):
            value = half[r, k]
            for d in range(1, at.wide):
                far_copy(r, k, d).wait_recv()
                value = value + far[r, d - 1, k]
            if mode:
                first = column[k * count : (k + 1) * count]
                value = value / jnp.where(mine == 0, first, column[(PIECES + k) * count : (PIECES + k + 1) * count])
            out[r, mine, k] = value
            back_copy(r, k).start()
        for k in range(PIECES):
            back_copy(r, k).wait_recv()

    q_size, q_wide = q.shape[4], q.shape[5]

    def qy_copy(r, j, e):
        return remote(q.at[r, j, :, (at.y + e) % at.flat], qy.at[r, j, e - 1], qy_s.at[r, j, e - 1], qy_r.at[r, j, e - 1], at.to_y(e))

    def hz_copy(r, j, d):
        return remote(h.at[r, j, (at.z + d) % at.deep], hz.at[r, j, d - 1], hz_s.at[r, j, d - 1], hz_r.at[r, j, d - 1], at.to_z(d))

    def multiply(r):
        ph[...], pw[...] = split(out[r].reshape(middle_rank, lines))

        def turn(j):
            columns = spread(j, q_wide)
            value = three(nn, (ph[...], pw[...]), (high[:, columns], low[:, columns]))
            q[r, j] = value.reshape(at.deep, at.flat, q_size, q_wide)
            for e in range(1, at.flat):
                qy_copy(r, j, e).start()

        loop(0, blocks, turn)

    def middle(r, j):
        value = q[r, j, :, pl.ds(at.y, 1)][:, 0]
        for e in range(1, at.flat):
            qy_copy(r, j, e).wait_recv()
            value = value + qy[r, j, e - 1]
        h[r, j] = value
        for d in range(1, at.deep):
            hz_copy(r, j, d).start()

    def last(r, j):
        value = h[r, j, pl.ds(at.z, 1)][0]
        for d in range(1, at.deep):
            hz_copy(r, j, d).wait_recv()
            value = value + hz[r, j, d - 1]
        chunk[r, :, spread(j, q_wide)] = value

    def add(r, u, value):
        product = three(nt, split(value), (high[:, lanes(u)], low[:, lanes(u)]))

        @pl.when(lanes_at(u) == 0)
        def _():
            if mode:
                part[r] = product.reshape(part.shape[1:])
            else:
                part[...] = product.reshape(part.shape)

        @pl.when(lanes_at(u) > 0)
        def _():
            if mode:
                part[r] = part[r] + product.reshape(part.shape[1:])
            else:
                part[...] = part[...] + product.reshape(part.shape)

    def lanes_at(u):
        return u % step_lanes if mode else u

    if mode == 0:
        count = m.shape[0] // units

        def divide(j):
            span = spread(j, count)
            high[span, :], low[span, :] = split(m[span, :] + g[span, :].astype(f32))

        loop(0, units, divide)
        forward(0)

        def turn(u):
            forward(u + 1)
            arrived(u)
            add(0, u, whole[u].reshape(rank, wide))

        loop(0, units - 1, turn)
        arrived(units - 1)
        add(0, jnp.int32(units - 1), whole[units - 1].reshape(rank, wide))
        join_begin(0)
        join_begin(1)
    else:
        work[...] = gram[...]
        x[...] = eye(rank)

        def step(u):
            factor_step(u, work, x, a, w)

            @pl.when(u > 0)
            def _():
                forward(u - 1)

        loop(0, units, step)
        xh[...], xl[...] = split(x[...])
        total[...] = jnp.zeros_like(total)

        def solve(r, u):
            arrived(u)
            span = slice(r * middle_rank, (r + 1) * middle_rank)
            s = jnp.zeros((middle_rank, wide), f32)
            for k in range(r + 1):
                columns = slice(k * middle_rank, (k + 1) * middle_rank)
                value = whole[u - (r - k) * step_lanes].reshape(middle_rank, wide)
                s = s + three(nn, (xh[span, columns], xl[span, columns]), split(value))
            sums = total[r]
            for k in range(0, wide, 128):
                sums = sums + s[:, k : k + 128] * s[:, k : k + 128]
            total[r] = sums
            add(r, u, s)

        loop(0, step_lanes, lambda u: solve(0, u))
        join_begin(0)
        forward(units - 1)
        loop(step_lanes, units, lambda u: solve(1, u))
        join_begin(1)

    join_end(0)
    multiply(0)
    middle(0, 0)
    join_end(1)
    own_rows = gram_own.shape[0]
    shares = PIECES * part.shape[3] // own_rows
    place = at.col // shares
    take = own_rows // part.shape[3]
    picked = out[place // CORES, place % CORES, pl.ds((at.col % shares) * take, take)].reshape(own_rows, lines)
    gram_own[...] = nt(picked, out[...].reshape(2 * middle_rank, lines), exact)
    share = gq.shape[2]
    for i in range(at.deep):
        for j in range(at.flat):
            k = (i * at.flat + j) * share
            gq[i, j] = gram_own[k : k + share, :]
    go = Sender(send, recv)
    gy = [go.start(gq.at[:, (at.y + e) % at.flat], gyr.at[e - 1], at.to_y(e)) for e in range(1, at.flat)]
    multiply(1)
    loop(1, blocks, lambda j: middle(0, j))
    value = gq[:, pl.ds(at.y, 1)][:, 0]
    for d, copy in enumerate(gy):
        copy.wait_recv()
        value = value + gyr[d]
    gh[...] = value
    gz = [go.start(gh.at[(at.z + d) % at.deep], gzr.at[d - 1], at.to_z(d)) for d in range(1, at.deep)]
    loop(0, blocks, lambda j: last(0, j))
    middle(1, 0)
    value = gh[pl.ds(at.z, 1)][0]
    for d, copy in enumerate(gz):
        copy.wait_recv()
        value = value + gzr[d]
    here = (at.x, at.core, at.z, at.y)
    gall[here] = value
    gz = [go.start(gall.at[here], gall.at[here], peer) for peer in at.z_peers()]
    loop(1, (blocks + 1) // 2, lambda j: middle(1, j))
    for copy in gz:
        copy.wait_recv()
    line_at = (at.x, at.core, slice(None), at.y)
    gy = [go.start(gall.at[line_at], gall.at[line_at], peer) for peer in at.y_peers()]
    loop((blocks + 1) // 2, blocks, lambda j: middle(1, j))
    for copy in gy:
        copy.wait_recv()
    gx = [go.start(gall.at[at.x, at.core], gall.at[at.x, at.core], peer) for peer in at.x_peers()]
    loop(0, blocks - 1, lambda j: last(1, j))
    for copy in gx:
        copy.wait_recv()
    gc = go.start(gall.at[:, at.core], gall.at[:, at.core], at.partner())
    last(1, blocks - 1)
    gc.wait_recv()
    go.drain()

    def finish(u):
        for d in range(1, at.deep):
            z_copy(u, d).wait_send()
        for e in range(1, at.flat):
            for d in range(at.deep):
                y_copy(u, e, d).wait_send()

    loop(0, units, finish)
    for r in range(2):
        for k in range(PIECES):
            near_copy(r, k).wait_send()
            back_copy(r, k).wait_send()
            for d in range(1, at.wide):
                far_copy(r, k, d).wait_send()
        if mode:
            for d in range(1, cols):
                sq_copy(r, d).wait_send()

        def sent(j):
            for e in range(1, at.flat):
                qy_copy(r, j, e).wait_send()
            for d in range(1, at.deep):
                hz_copy(r, j, d).wait_send()

        loop(0, blocks, sent)


def iterate(mode, rows, cols, ident, own, *args):
    width = own.shape[-1]
    lines = args[-1].shape[0]
    rank = own.size // width * rows
    deep = outer_factor(rows)
    flat = rows // deep
    xs = cols // CORES
    units = 4
    size = rank // rows // (2 if mode else 1)
    wide = width // units * (2 if mode else 1)
    blocks = max(1, min(4, width // 256))
    half_rank, q_wide, q_size = rank // 2, width // blocks, rank // rows // 2
    piece = half_rank // (CORES * PIECES)
    share = rank // cols // rows
    dma = pltpu.SemaphoreType.DMA
    out_shape = [
        jax.ShapeDtypeStruct((2, CORES, PIECES, piece, lines), f32),
        jax.ShapeDtypeStruct((2, q_size, width), f32),
        jax.ShapeDtypeStruct((xs, CORES, deep, flat, share, rank), f32),
    ]
    scratch = []
    if mode == 0:
        out_shape = [jax.ShapeDtypeStruct((lines, width), bf16)] * 2 + out_shape
    else:
        block = rank // units
        scratch = [pltpu.VMEM((rank, rank), f32)] + [pltpu.VMEM((rank, rank), bf16)] * 2
        scratch += [pltpu.VMEM((block, block), f32)] * 2 + [pltpu.VMEM((rank, rank), f32), pltpu.VMEM((2, half_rank, 128), f32)]
        scratch += [pltpu.VMEM((2, 8, half_rank), f32), pltpu.VMEM((2, cols - 1, 8, half_rank), f32)]
        scratch += [dma((2, cols - 1))] * 2
    scratch += [
        pltpu.VMEM((units, deep, flat, size, wide), f32),
        pltpu.VMEM((2, CORES, PIECES, piece, lines), f32),
        pltpu.VMEM((2, PIECES, piece, lines), f32),
        pltpu.VMEM((2, PIECES, piece, lines), f32),
        pltpu.VMEM((2, xs - 1, PIECES, piece, lines), f32),
        pltpu.VMEM((rank // cols, rank), f32),
        pltpu.VMEM((half_rank, lines), bf16),
        pltpu.VMEM((half_rank, lines), bf16),
        pltpu.VMEM((2, blocks, deep, flat, q_size, q_wide), f32),
        pltpu.VMEM((2, blocks, flat - 1, deep, q_size, q_wide), f32),
        pltpu.VMEM((2, blocks, deep, q_size, q_wide), f32),
        pltpu.VMEM((2, blocks, deep - 1, q_size, q_wide), f32),
        pltpu.VMEM((deep, flat, share, rank), f32),
        pltpu.VMEM((flat - 1, deep, share, rank), f32),
        pltpu.VMEM((deep, share, rank), f32),
        pltpu.VMEM((deep - 1, share, rank), f32),
    ]
    scratch += [dma((units, deep - 1))] * 2 + [dma((units, flat - 1, deep))] * 2
    scratch += [dma((2, PIECES))] * 2 + [dma((2, PIECES, xs - 1))] * 2 + [dma((2, PIECES))] * 2
    scratch += [dma((2, blocks, flat - 1))] * 2 + [dma((2, blocks, deep - 1))] * 2
    scratch += [dma((2 * (deep - 1) + 2 * (flat - 1) + xs,))] * 2
    res = pl.pallas_call(
        functools.partial(iterate_kernel, rows, cols, units, blocks, mode),
        name="iterate",
        out_shape=out_shape,
        in_specs=[VMEM] * (1 + len(args)),
        out_specs=[VMEM] * len(out_shape),
        scratch_shapes=scratch,
        compiler_params=pltpu.CompilerParams(collective_id=ident, has_side_effects=True, vmem_limit_bytes=LIMIT),
        cost_estimate=cost(6e10, 24 << 20),
    )(own, *args)
    joined, chunk, gall = res[-3:]
    return list(res[:-3]) + [joined.reshape(rank, lines), chunk, gall.reshape(rank, rank)]


def gather_kernel(rows, cols, blocks, *refs):
    own, gram, p, solved, norms, left_high, left_low = refs[:7]
    whole, x, xh, xl, a, w, work, total, sq, sq_in, ss, sr, zs, zr, ys, yr = refs[7:]
    at = Place(rows, cols)
    col_peers = [(at.row, (at.col + d) % cols) for d in range(1, cols)]
    greet(at.y_peers() + at.z_peers() + col_peers)
    wide, size = whole.shape[-1], own.shape[0]
    rank = size * rows

    def lanes(j):
        if isinstance(j, int):
            return slice(j * wide, (j + 1) * wide)
        return pl.ds(pl.multiple_of(j * wide, wide), wide)

    def z_copy(j, d):
        return pltpu.make_async_remote_copy(
            src_ref=own.at[:, lanes(j)],
            dst_ref=whole.at[j, at.z, at.y],
            send_sem=zs.at[j, d - 1],
            recv_sem=zr.at[j, d - 1],
            device_id=at.to_z(d),
            device_id_type=MESH,
        )

    def y_copy(j, e, d):
        chunk = whole.at[j, (at.z - d + at.deep) % at.deep, at.y]
        return pltpu.make_async_remote_copy(
            src_ref=own.at[:, lanes(j)] if d == 0 else chunk,
            dst_ref=chunk,
            send_sem=ys.at[j, e - 1, d],
            recv_sem=yr.at[j, e - 1, d],
            device_id=at.to_y(e),
            device_id_type=MESH,
        )

    for j in range(blocks):
        for d in range(1, at.deep):
            z_copy(j, d).start()
        for e in range(1, at.flat):
            y_copy(j, e, 0).start()
    for j in range(blocks):
        whole[j, at.z, at.y] = own[:, lanes(j)]

    def forward(j):
        for d in range(1, at.deep):
            z_copy(j, d).wait_recv()
            for e in range(1, at.flat):
                y_copy(j, e, d).start()

    def block(j):
        for e in range(1, at.flat):
            for d in range(at.deep):
                y_copy(j, e, d).wait_recv()
        return jnp.swapaxes(whole[j].reshape(rows, 2, size // 2, wide), 0, 1).reshape(rank, wide)

    def loop(count, body):
        lax.fori_loop(0, count, lambda j, c: (body(j), c)[1], 0)

    work[...] = gram[...]
    x[...] = eye(rank)

    def step(j):
        factor_step(j, work, x, a, w)

        @pl.when(j > 0)
        def _():
            forward(j - 1)

    loop(blocks, step)
    xh[...], xl[...] = split(x[...])
    lines = min(256, p.shape[1])

    def left(i):
        span = pl.ds(pl.multiple_of(i * lines, lines), lines)
        value = three(nn, (xh[...], xl[...]), split(p[:, span])).T
        left_high[span, :], left_low[span, :] = split(value)

    loop(p.shape[1] // lines, left)
    total[...] = jnp.zeros_like(total)

    def turn(j):
        s = three(nn, (xh[...], xl[...]), split(block(j)))
        sums = total[...]
        for k in range(0, wide, 128):
            sums = sums + s[:, k : k + 128] * s[:, k : k + 128]
        total[...] = sums
        solved[:, lanes(j)] = s

        @pl.when(j == min(1, blocks - 1))
        def _():
            forward(blocks - 1)

    if blocks == 1:
        forward(0)
    loop(blocks, turn)
    sq[...] = row_sums(total[...])
    go = Sender(ss, sr)
    copies = [go.start(sq, sq_in.at[d], peer) for d, peer in enumerate(col_peers)]
    value = sq[...]
    for d, copy in enumerate(copies):
        copy.wait_recv()
        value = value + sq_in[d]
    norms[...] = jnp.sqrt(value + epsilon)
    go.drain()
    for j in range(blocks):
        for d in range(1, at.deep):
            z_copy(j, d).wait_send()
        for e in range(1, at.flat):
            for d in range(at.deep):
                y_copy(j, e, d).wait_send()


def gather(rows, cols, ident, own, gram, p):
    size, width = own.shape
    rank, lines = p.shape
    blocks = max(1, min(4, width // 256, rank // 128))
    deep = outer_factor(rows)
    flat = rows // deep
    block = rank // blocks
    dma = pltpu.SemaphoreType.DMA
    out_shape = [jax.ShapeDtypeStruct((rank, width), f32), jax.ShapeDtypeStruct((8, rank), f32)]
    out_shape += [jax.ShapeDtypeStruct((lines, rank), bf16)] * 2
    scratch = [pltpu.VMEM((blocks, deep, flat, size, width // blocks), f32)]
    scratch += [pltpu.VMEM((rank, rank), f32)] + [pltpu.VMEM((rank, rank), bf16)] * 2
    scratch += [pltpu.VMEM((block, block), f32)] * 2 + [pltpu.VMEM((rank, rank), f32), pltpu.VMEM((rank, 128), f32)]
    scratch += [pltpu.VMEM((8, rank), f32), pltpu.VMEM((cols - 1, 8, rank), f32)] + [dma((cols - 1,))] * 2
    scratch += [dma((blocks, deep - 1))] * 2 + [dma((blocks, flat - 1, deep))] * 2
    return pl.pallas_call(
        functools.partial(gather_kernel, rows, cols, blocks),
        name="gather",
        out_shape=out_shape,
        in_specs=[VMEM] * 3,
        out_specs=[VMEM] * len(out_shape),
        scratch_shapes=scratch,
        compiler_params=pltpu.CompilerParams(collective_id=ident, has_side_effects=True, vmem_limit_bytes=LIMIT),
        cost_estimate=cost(3e10, 16 << 20),
    )(own, gram, p)


def shards(rows, cols, momentum, gradient, weight, right_start):
    out_dim, in_dim = momentum.shape[0] * rows, momentum.shape[1] * cols
    rank = right_start.shape[1] * rows
    high, low, joined, own, gram = iterate(0, rows, cols, 0, right_start.T, momentum, gradient)
    for iteration in range(1, ITERS):
        joined, own, gram = iterate(1, rows, cols, 1, own, gram, high, low)
    own = own.reshape(rank // rows, own.shape[-1])
    products, norms, left_high, left_low = gather(rows, cols, 2, own, gram, joined)
    scale_factor = step_rate * (out_dim * in_dim / rank) ** 0.5
    new_momentum, new_weight = outputs(scale_factor, left_high, left_low, products, norms, momentum, gradient, weight)
    size = rank // rows
    start = lax.axis_index("row") * size
    some = lax.dynamic_slice_in_dim(products, start, size, axis=0)
    norm = lax.dynamic_slice_in_dim(norms[0], start, size, axis=0)
    return new_momentum, new_weight, (some / norm[:, None]).T


def solution(mesh):
    rows, cols = mesh.shape["row"], mesh.shape["col"]
    return jax.shard_map(
        functools.partial(shards, rows, cols),
        mesh=mesh,
        in_specs=(P("row", "col"), P("row", "col"), P("row", "col"), P("col", "row")),
        out_specs=(P("row", "col"), P("row", "col"), P("col", "row")),
        check_vma=False,
    )
```

```python
import functools

import jax
import jax.numpy as jnp
from jax import lax
from jax.experimental import pallas as pl
from jax.experimental.pallas import tpu as pltpu
from jax.sharding import PartitionSpec as P

ITERS = 2
CORES = 2
momentum_decay = 0.9
step_rate = 0.1
epsilon = 1e-06
exact = lax.Precision.HIGHEST
f32, bf16 = jnp.float32, jnp.bfloat16
VMEM = pl.BlockSpec(memory_space=pltpu.VMEM)
FAR = pl.BlockSpec(memory_space=pl.ANY)
MESH = pl.DeviceIdType.MESH
LIMIT = 56 << 20


def nt(a, b, precision=None):
    return lax.dot_general(a, b, (((1,), (1,)), ((), ())), precision=precision, preferred_element_type=f32)


def nn(a, b, precision=None):
    return lax.dot_general(a, b, (((1,), (0,)), ((), ())), precision=precision, preferred_element_type=f32)


def split(x):
    high = x.astype(bf16)
    return high, (x - high.astype(f32)).astype(bf16)


def three(dot, a, b):
    return (dot(a[1], b[0]) + dot(a[0], b[1])) + dot(a[0], b[0])


def outer_factor(n):
    d = 1
    while d * d < n or n % d:
        d += 1
    return d


def cost(flops, moved):
    return pl.CostEstimate(flops=int(flops), bytes_accessed=int(moved), transcendentals=0)


def eye(n):
    return (lax.broadcasted_iota(jnp.int32, (n, n), 0) == lax.broadcasted_iota(jnp.int32, (n, n), 1)).astype(f32)


def eliminate(a, w):
    size = a.shape[0]
    shape = (8, size)
    sub = lax.broadcasted_iota(jnp.int32, shape, 0)
    w[...] = eye(size)
    for at in range(0, size, 8):
        slab, inv_rows = a[at : at + 8, :], w[at : at + 8, :]
        cols = [jnp.broadcast_to(slab[:, at + i : at + i + 1], shape) for i in range(8)]
        scale = jnp.zeros(shape, f32)
        for i in range(8):
            pivot = jnp.broadcast_to(cols[i][i : i + 1, :], shape)
            scale = jnp.where(sub == i, lax.rsqrt(pivot), scale)
            if i < 7:
                m = jnp.where(sub > i, cols[i] / pivot, 0.0)
                for k in range(i + 1, 8):
                    cols[k] = cols[k] - m * jnp.broadcast_to(cols[k][i : i + 1, :], shape)
                slab = slab - m * jnp.broadcast_to(slab[i : i + 1, :], shape)
                inv_rows = inv_rows - m * jnp.broadcast_to(inv_rows[i : i + 1, :], shape)
        upper, inv_rows = slab * scale, inv_rows * scale
        w[at : at + 8, :] = inv_rows
        lower = upper.T
        for k in range(at + 8, size, 8):
            rows, inv = a[k : k + 8, :], w[k : k + 8, :]
            for i in range(8):
                factor = jnp.broadcast_to(lower[k : k + 8, i : i + 1], shape)
                rows = rows - factor * jnp.broadcast_to(upper[i : i + 1, :], shape)
                inv = inv - factor * jnp.broadcast_to(inv_rows[i : i + 1, :], shape)
            a[k : k + 8, :] = rows
            w[k : k + 8, :] = inv


def factor_step(step, work, x, a, w):
    rank, block = work.shape[0], a.shape[0]
    span = pl.ds(pl.multiple_of(step * block, block), block)
    a[...] = work[span, span]
    eliminate(a, w)
    inverse = w[...]
    below = lax.broadcasted_iota(jnp.int32, (rank, block), 0) >= (step + 1) * block
    panel = jnp.where(below, nt(work[:, span], inverse, exact), 0.0)
    solved = nn(inverse, x[span, :], exact)
    x[...] = x[...] - nn(panel, solved, exact)
    x[span, :] = solved
    work[...] = work[...] - nt(panel, panel, exact)


def row_sums(total):
    rank = total.shape[0]
    column = jnp.sum(total, axis=1, keepdims=True)
    return jnp.broadcast_to(column, (rank, 128)).T[:8, :]


def final_kernel(scale_factor, high, low, q, norms, m, g, weight, new_m, new_w, new_r, scaled):
    rank = q.shape[0]
    column = jnp.broadcast_to(norms[0:1, :], (128, rank)).T[:, 0:1]
    s = q[...]
    left = (high[...], low[...])
    blended = m[...] + g[...].astype(f32)
    new_m[...] = blended - (1.0 - momentum_decay) * nn(left[0], s.astype(bf16))
    right = s / column
    scaled[...] = right
    size = new_r.shape[0]
    new_r[...] = scaled[pl.ds(pl.multiple_of(lax.axis_index("row") * size, size), size), :]
    update = three(nn, left, split(right))
    new_w[...] = (weight[...].astype(f32) - scale_factor * update).astype(bf16)


def outputs(scale_factor, size, high, low, q, norms, momentum, gradient, weight):
    rank, cols = q.shape
    rows = high.shape[0]
    wide = min(256, cols)
    side = pl.BlockSpec((rows, rank), lambda j: (0, 0))
    block = pl.BlockSpec((rows, wide), lambda j: (0, j))
    return pl.pallas_call(
        functools.partial(final_kernel, scale_factor),
        name="outputs",
        grid=(cols // wide,),
        in_specs=[side, side, pl.BlockSpec((rank, wide), lambda j: (0, j)), pl.BlockSpec((8, rank), lambda j: (0, 0)), block, block, block],
        out_specs=[block, block, pl.BlockSpec((size, wide), lambda j: (0, j))],
        out_shape=[
            jax.ShapeDtypeStruct((rows, cols), f32),
            jax.ShapeDtypeStruct((rows, cols), bf16),
            jax.ShapeDtypeStruct((size, cols), f32),
        ],
        scratch_shapes=[pltpu.VMEM((rank, wide), f32)],
        compiler_params=pltpu.CompilerParams(vmem_limit_bytes=LIMIT),
        cost_estimate=cost(8 * rank * rows * cols, 14 * rows * cols),
    )(high, low, q, norms, momentum, gradient, weight)


class Place:
    def __init__(self, rows, cols):
        self.deep = outer_factor(rows)
        self.flat = rows // self.deep
        self.wide = cols // CORES
        self.row, self.col = lax.axis_index("row"), lax.axis_index("col")
        self.z, self.y = self.row // self.flat, self.row % self.flat
        self.x, self.core = self.col // CORES, self.col % CORES

    def to_y(self, d):
        return (self.z * self.flat + (self.y + d) % self.flat, self.col)

    def to_z(self, d):
        return (((self.z + d) % self.deep) * self.flat + self.y, self.col)

    def to_x(self, d):
        return (self.row, ((self.x + d) % self.wide) * CORES + self.core)

    def partner(self):
        return (self.row, self.x * CORES + 1 - self.core)

    def y_peers(self):
        return [self.to_y(d) for d in range(1, self.flat)]

    def z_peers(self):
        return [self.to_z(d) for d in range(1, self.deep)]

    def x_peers(self):
        return [self.to_x(d) for d in range(1, self.wide)]


def greet(peers):
    barrier = pltpu.get_barrier_semaphore()
    for peer in peers:
        pl.semaphore_signal(barrier, inc=1, device_id=peer, device_id_type=MESH)
    pl.semaphore_wait(barrier, len(peers))


class Sender:
    def __init__(self, send, recv):
        self.send, self.recv, self.copies = send, recv, []

    def start(self, src, dst, peer):
        at = len(self.copies)
        copy = pltpu.make_async_remote_copy(
            src_ref=src, dst_ref=dst, send_sem=self.send.at[at], recv_sem=self.recv.at[at], device_id=peer, device_id_type=MESH
        )
        copy.start()
        self.copies.append(copy)
        return copy

    def drain(self):
        for copy in self.copies:
            copy.wait_send()


PIECES = 4


def iterate_kernel(rows, cols, units, blocks, mode, *refs):
    if mode == 0:
        own, m_far, g_far, high_far, low_far, out, chunk, gall = refs[:8]
        m, g, high, low, in_sem, out_sem = refs[8:14]
        refs = refs[14:]
    else:
        own, gram, high_far, low_far, out, chunk, gall = refs[:7]
        x, xh, xl, a, w, work, total, sq, sq_in, ss, sr, high, low, in_sem = refs[7:21]
        refs = refs[21:]
    whole, part, half, near, far, gram_own, ph, pw, q, qy, h, hz, gq, gyr, gh, gzr, zs, zr, ys, yr = refs[:20]
    join_s, join_r, far_s, far_r, back_s, back_r, qy_s, qy_r, hz_s, hz_r, send, recv = refs[20:]
    at = Place(rows, cols)
    peers = at.y_peers() + at.z_peers()
    col_peers = [(at.row, (at.col + d) % cols) for d in range(1, cols)]
    greet(peers + (col_peers if mode else at.x_peers() + [at.partner()]))
    size, wide = whole.shape[3], whole.shape[4]
    rank, middle_rank = size * rows * (2 if mode else 1), part.shape[1] * part.shape[2] * part.shape[3]
    lines = part.shape[-1]
    step_lanes = units // 2

    def remote(src, dst, send_sem, recv_sem, peer):
        return pltpu.make_async_remote_copy(
            src_ref=src, dst_ref=dst, send_sem=send_sem, recv_sem=recv_sem, device_id=peer, device_id_type=MESH
        )

    def spread(at_index, count):
        if isinstance(at_index, int):
            return slice(at_index * count, (at_index + 1) * count)
        return pl.ds(pl.multiple_of(at_index * count, count), count)

    def loop(start, count, body):
        lax.fori_loop(start, count, lambda j, c: (body(j), c)[1], 0)

    split_lines = high.shape[0] // units

    def fetch(j):
        span = spread(j, split_lines)
        pairs = ((m_far, m), (g_far, g)) if mode == 0 else ((high_far, high), (low_far, low))
        return [pltpu.make_async_copy(src.at[span], dst.at[span], in_sem.at[j, i]) for i, (src, dst) in enumerate(pairs)]

    def keep(j):
        span = spread(j, split_lines)
        pairs = ((high, high_far), (low, low_far))
        return [pltpu.make_async_copy(src.at[span], dst.at[span], out_sem.at[j, i]) for i, (src, dst) in enumerate(pairs)]

    def lanes(u):
        return spread(u % step_lanes, wide) if mode else spread(u, wide)

    def source(u):
        return own.at[u // step_lanes, :, lanes(u)] if mode else own.at[:, lanes(u)]

    def z_copy(u, d):
        return remote(source(u), whole.at[u, at.z, at.y], zs.at[u, d - 1], zr.at[u, d - 1], at.to_z(d))

    def y_copy(u, e, d):
        piece = whole.at[u, (at.z - d + at.deep) % at.deep, at.y]
        return remote(source(u) if d == 0 else piece, piece, ys.at[u, e - 1, d], yr.at[u, e - 1, d], at.to_y(e))

    for u in range(units):
        for d in range(1, at.deep):
            z_copy(u, d).start()
        for e in range(1, at.flat):
            y_copy(u, e, 0).start()
    for u in range(units):
        for copy in fetch(u):
            copy.start()
    for u in range(units):
        whole[u, at.z, at.y] = own[u // step_lanes, :, lanes(u)] if mode else own[:, lanes(u)]

    def forward(u):
        for d in range(1, at.deep):
            z_copy(u, d).wait_recv()
            for e in range(1, at.flat):
                y_copy(u, e, d).start()

    def arrived(u):
        for e in range(1, at.flat):
            for d in range(at.deep):
                y_copy(u, e, d).wait_recv()

    mine, other = at.core, 1 - at.core

    def near_copy(r, k):
        return remote(part.at[r, other, k], near.at[r, k], join_s.at[r, k], join_r.at[r, k], at.partner())

    def far_copy(r, k, d):
        return remote(half.at[r, k], far.at[r, d - 1, k], far_s.at[r, k, d - 1], far_r.at[r, k, d - 1], at.to_x(d))

    def back_copy(r, k):
        return remote(out.at[r, mine, k], out.at[r, mine, k], back_s.at[r, k], back_r.at[r, k], at.partner())

    def sq_copy(r, d):
        return remote(sq.at[r], sq_in.at[r, d - 1], ss.at[r, d - 1], sr.at[r, d - 1], (at.row, (at.col + d) % cols))

    def join_begin(r):
        if mode:
            sq[r] = row_sums(total[r])
            for d in range(1, cols):
                sq_copy(r, d).start()
        for k in range(PIECES):
            near_copy(r, k).start()
        for k in range(PIECES):
            near_copy(r, k).wait_recv()
            half[r, k] = part[r, mine, k] + near[r, k]
            for d in range(1, at.wide):
                far_copy(r, k, d).start()

    def join_end(r):
        if mode:
            value = sq[r]
            for d in range(1, cols):
                sq_copy(r, d).wait_recv()
                value = value + sq_in[r, d - 1]
            norm = jnp.sqrt(value + epsilon)
            column = jnp.broadcast_to(norm[0:1, :], (128, middle_rank)).T[:, 0:1]
            count = middle_rank // (CORES * PIECES)
        for k in range(PIECES):
            value = half[r, k]
            for d in range(1, at.wide):
                far_copy(r, k, d).wait_recv()
                value = value + far[r, d - 1, k]
            if mode:
                first = column[k * count : (k + 1) * count]
                value = value / jnp.where(mine == 0, first, column[(PIECES + k) * count : (PIECES + k + 1) * count])
            out[r, mine, k] = value
            back_copy(r, k).start()
        for k in range(PIECES):
            back_copy(r, k).wait_recv()

    q_size, q_wide = q.shape[4], q.shape[5]

    def qy_copy(r, j, e):
        return remote(q.at[r, j, :, (at.y + e) % at.flat], qy.at[r, j, e - 1], qy_s.at[r, j, e - 1], qy_r.at[r, j, e - 1], at.to_y(e))

    def hz_copy(r, j, d):
        return remote(h.at[r, j, (at.z + d) % at.deep], hz.at[r, j, d - 1], hz_s.at[r, j, d - 1], hz_r.at[r, j, d - 1], at.to_z(d))

    def multiply(r):
        ph[...], pw[...] = split(out[r].reshape(middle_rank, lines))

        def turn(j):
            columns = spread(j, q_wide)
            value = three(nn, (ph[...], pw[...]), (high[:, columns], low[:, columns]))
            q[r, j] = value.reshape(at.deep, at.flat, q_size, q_wide)
            for e in range(1, at.flat):
                qy_copy(r, j, e).start()

        loop(0, blocks, turn)

    def middle(r, j):
        value = q[r, j, :, pl.ds(at.y, 1)][:, 0]
        for e in range(1, at.flat):
            qy_copy(r, j, e).wait_recv()
            value = value + qy[r, j, e - 1]
        h[r, j] = value
        for d in range(1, at.deep):
            hz_copy(r, j, d).start()

    def last(r, j):
        value = h[r, j, pl.ds(at.z, 1)][0]
        for d in range(1, at.deep):
            hz_copy(r, j, d).wait_recv()
            value = value + hz[r, j, d - 1]
        chunk[r, :, spread(j, q_wide)] = value

    def add(r, u, value):
        product = three(nt, split(value), (high[:, lanes(u)], low[:, lanes(u)]))

        @pl.when(lanes_at(u) == 0)
        def _():
            if mode:
                part[r] = product.reshape(part.shape[1:])
            else:
                part[...] = product.reshape(part.shape)

        @pl.when(lanes_at(u) > 0)
        def _():
            if mode:
                part[r] = part[r] + product.reshape(part.shape[1:])
            else:
                part[...] = part[...] + product.reshape(part.shape)

    def lanes_at(u):
        return u % step_lanes if mode else u

    if mode == 0:
        def divide(j):
            span = spread(j, split_lines)
            for copy in fetch(j):
                copy.wait()
            high[span, :], low[span, :] = split(m[span, :] + g[span, :].astype(f32))
            for copy in keep(j):
                copy.start()

        loop(0, units, divide)
        forward(0)

        def turn(u):
            forward(u + 1)
            arrived(u)
            add(0, u, whole[u].reshape(rank, wide))

        loop(0, units - 1, turn)
        arrived(units - 1)
        add(0, jnp.int32(units - 1), whole[units - 1].reshape(rank, wide))
        join_begin(0)
        join_begin(1)
    else:
        work[...] = gram[...]
        x[...] = eye(rank)

        def step(u):
            factor_step(u, work, x, a, w)

            @pl.when(u > 0)
            def _():
                forward(u - 1)

        loop(0, units, step)
        xh[...], xl[...] = split(x[...])
        total[...] = jnp.zeros_like(total)
        for u in range(units):
            for copy in fetch(u):
                copy.wait()

        def solve(r, u):
            arrived(u)
            span = slice(r * middle_rank, (r + 1) * middle_rank)
            s = jnp.zeros((middle_rank, wide), f32)
            for k in range(r + 1):
                columns = slice(k * middle_rank, (k + 1) * middle_rank)
                value = whole[u - (r - k) * step_lanes].reshape(middle_rank, wide)
                s = s + three(nn, (xh[span, columns], xl[span, columns]), split(value))
            sums = total[r]
            for k in range(0, wide, 128):
                sums = sums + s[:, k : k + 128] * s[:, k : k + 128]
            total[r] = sums
            add(r, u, s)

        loop(0, step_lanes, lambda u: solve(0, u))
        join_begin(0)
        forward(units - 1)
        loop(step_lanes, units, lambda u: solve(1, u))
        join_begin(1)

    join_end(0)
    multiply(0)
    middle(0, 0)
    join_end(1)
    own_rows = gram_own.shape[0]
    shares = PIECES * part.shape[3] // own_rows
    place = at.col // shares
    take = own_rows // part.shape[3]
    picked = out[place // CORES, place % CORES, pl.ds((at.col % shares) * take, take)].reshape(own_rows, lines)
    gram_own[...] = nt(picked, out[...].reshape(2 * middle_rank, lines), exact)
    share = gq.shape[2]
    for i in range(at.deep):
        for j in range(at.flat):
            k = (i * at.flat + j) * share
            gq[i, j] = gram_own[k : k + share, :]
    go = Sender(send, recv)
    gy = [go.start(gq.at[:, (at.y + e) % at.flat], gyr.at[e - 1], at.to_y(e)) for e in range(1, at.flat)]
    multiply(1)
    loop(1, blocks, lambda j: middle(0, j))
    value = gq[:, pl.ds(at.y, 1)][:, 0]
    for d, copy in enumerate(gy):
        copy.wait_recv()
        value = value + gyr[d]
    gh[...] = value
    gz = [go.start(gh.at[(at.z + d) % at.deep], gzr.at[d - 1], at.to_z(d)) for d in range(1, at.deep)]
    loop(0, blocks, lambda j: last(0, j))
    middle(1, 0)
    value = gh[pl.ds(at.z, 1)][0]
    for d, copy in enumerate(gz):
        copy.wait_recv()
        value = value + gzr[d]
    here = (at.x, at.core, at.z, at.y)
    gall[here] = value
    gz = [go.start(gall.at[here], gall.at[here], peer) for peer in at.z_peers()]
    loop(1, (blocks + 1) // 2, lambda j: middle(1, j))
    for copy in gz:
        copy.wait_recv()
    line_at = (at.x, at.core, slice(None), at.y)
    gy = [go.start(gall.at[line_at], gall.at[line_at], peer) for peer in at.y_peers()]
    loop((blocks + 1) // 2, blocks, lambda j: middle(1, j))
    for copy in gy:
        copy.wait_recv()
    gx = [go.start(gall.at[at.x, at.core], gall.at[at.x, at.core], peer) for peer in at.x_peers()]
    loop(0, blocks - 1, lambda j: last(1, j))
    for copy in gx:
        copy.wait_recv()
    gc = go.start(gall.at[:, at.core], gall.at[:, at.core], at.partner())
    last(1, blocks - 1)
    gc.wait_recv()
    go.drain()

    def finish(u):
        if mode == 0:
            for copy in keep(u):
                copy.wait()
        for d in range(1, at.deep):
            z_copy(u, d).wait_send()
        for e in range(1, at.flat):
            for d in range(at.deep):
                y_copy(u, e, d).wait_send()

    loop(0, units, finish)
    for r in range(2):
        for k in range(PIECES):
            near_copy(r, k).wait_send()
            back_copy(r, k).wait_send()
            for d in range(1, at.wide):
                far_copy(r, k, d).wait_send()
        if mode:
            for d in range(1, cols):
                sq_copy(r, d).wait_send()

        def sent(j):
            for e in range(1, at.flat):
                qy_copy(r, j, e).wait_send()
            for d in range(1, at.deep):
                hz_copy(r, j, d).wait_send()

        loop(0, blocks, sent)


def iterate(mode, rows, cols, ident, own, *args):
    width = own.shape[-1]
    lines = args[-1].shape[0]
    rank = own.size // width * rows
    deep = outer_factor(rows)
    flat = rows // deep
    xs = cols // CORES
    units = 4
    size = rank // rows // (2 if mode else 1)
    wide = width // units * (2 if mode else 1)
    blocks = max(1, min(4, width // 256))
    half_rank, q_wide, q_size = rank // 2, width // blocks, rank // rows // 2
    piece = half_rank // (CORES * PIECES)
    share = rank // cols // rows
    dma = pltpu.SemaphoreType.DMA
    out_shape = [
        jax.ShapeDtypeStruct((2, CORES, PIECES, piece, lines), f32),
        jax.ShapeDtypeStruct((2, q_size, width), f32),
        jax.ShapeDtypeStruct((xs, CORES, deep, flat, share, rank), f32),
    ]
    scratch = []
    if mode == 0:
        out_shape = [jax.ShapeDtypeStruct((lines, width), bf16)] * 2 + out_shape
        scratch = [pltpu.VMEM((lines, width), dtype) for dtype in (f32, bf16, bf16, bf16)] + [dma((units, 2))] * 2
    else:
        block = rank // units
        scratch = [pltpu.VMEM((rank, rank), f32)] + [pltpu.VMEM((rank, rank), bf16)] * 2
        scratch += [pltpu.VMEM((block, block), f32)] * 2 + [pltpu.VMEM((rank, rank), f32), pltpu.VMEM((2, half_rank, 128), f32)]
        scratch += [pltpu.VMEM((2, 8, half_rank), f32), pltpu.VMEM((2, cols - 1, 8, half_rank), f32)]
        scratch += [dma((2, cols - 1))] * 2
        scratch += [pltpu.VMEM((lines, width), bf16)] * 2 + [dma((units, 2))]
    scratch += [
        pltpu.VMEM((units, deep, flat, size, wide), f32),
        pltpu.VMEM((2, CORES, PIECES, piece, lines), f32),
        pltpu.VMEM((2, PIECES, piece, lines), f32),
        pltpu.VMEM((2, PIECES, piece, lines), f32),
        pltpu.VMEM((2, xs - 1, PIECES, piece, lines), f32),
        pltpu.VMEM((rank // cols, rank), f32),
        pltpu.VMEM((half_rank, lines), bf16),
        pltpu.VMEM((half_rank, lines), bf16),
        pltpu.VMEM((2, blocks, deep, flat, q_size, q_wide), f32),
        pltpu.VMEM((2, blocks, flat - 1, deep, q_size, q_wide), f32),
        pltpu.VMEM((2, blocks, deep, q_size, q_wide), f32),
        pltpu.VMEM((2, blocks, deep - 1, q_size, q_wide), f32),
        pltpu.VMEM((deep, flat, share, rank), f32),
        pltpu.VMEM((flat - 1, deep, share, rank), f32),
        pltpu.VMEM((deep, share, rank), f32),
        pltpu.VMEM((deep - 1, share, rank), f32),
    ]
    scratch += [dma((units, deep - 1))] * 2 + [dma((units, flat - 1, deep))] * 2
    scratch += [dma((2, PIECES))] * 2 + [dma((2, PIECES, xs - 1))] * 2 + [dma((2, PIECES))] * 2
    scratch += [dma((2, blocks, flat - 1))] * 2 + [dma((2, blocks, deep - 1))] * 2
    scratch += [dma((2 * (deep - 1) + 2 * (flat - 1) + xs,))] * 2
    res = pl.pallas_call(
        functools.partial(iterate_kernel, rows, cols, units, blocks, mode),
        name="iterate",
        out_shape=out_shape,
        in_specs=[VMEM] * (len(args) - 1) + [FAR] * 2,
        out_specs=[FAR] * (len(out_shape) - 3) + [VMEM] * 3,
        scratch_shapes=scratch,
        compiler_params=pltpu.CompilerParams(collective_id=ident, has_side_effects=True, vmem_limit_bytes=LIMIT),
        cost_estimate=cost(6e10, 24 << 20),
    )(own, *args)
    joined, chunk, gall = res[-3:]
    return list(res[:-3]) + [joined.reshape(rank, lines), chunk, gall.reshape(rank, rank)]


def gather_kernel(rows, cols, blocks, *refs):
    own, gram, p_far, solved_far, norms, left_high_far, left_low_far = refs[:7]
    whole, x, xh, xl, a, w, work, total, sq, sq_in, ss, sr = refs[7:19]
    p, solved, left_high, left_low, p_sem, solved_sem, left_sem, zs, zr, ys, yr = refs[19:]
    at = Place(rows, cols)
    col_peers = [(at.row, (at.col + d) % cols) for d in range(1, cols)]
    greet(at.y_peers() + at.z_peers() + col_peers)
    wide, size = whole.shape[-1], own.shape[0]
    rank = size * rows

    def lanes(j):
        if isinstance(j, int):
            return slice(j * wide, (j + 1) * wide)
        return pl.ds(pl.multiple_of(j * wide, wide), wide)

    def z_copy(j, d):
        return pltpu.make_async_remote_copy(
            src_ref=own.at[:, lanes(j)],
            dst_ref=whole.at[j, at.z, at.y],
            send_sem=zs.at[j, d - 1],
            recv_sem=zr.at[j, d - 1],
            device_id=at.to_z(d),
            device_id_type=MESH,
        )

    def y_copy(j, e, d):
        chunk = whole.at[j, (at.z - d + at.deep) % at.deep, at.y]
        return pltpu.make_async_remote_copy(
            src_ref=own.at[:, lanes(j)] if d == 0 else chunk,
            dst_ref=chunk,
            send_sem=ys.at[j, e - 1, d],
            recv_sem=yr.at[j, e - 1, d],
            device_id=at.to_y(e),
            device_id_type=MESH,
        )

    for j in range(blocks):
        for d in range(1, at.deep):
            z_copy(j, d).start()
        for e in range(1, at.flat):
            y_copy(j, e, 0).start()
    fetch = pltpu.make_async_copy(p_far, p, p_sem.at[0])
    fetch.start()
    for j in range(blocks):
        whole[j, at.z, at.y] = own[:, lanes(j)]

    def forward(j):
        for d in range(1, at.deep):
            z_copy(j, d).wait_recv()
            for e in range(1, at.flat):
                y_copy(j, e, d).start()

    def block(j):
        for e in range(1, at.flat):
            for d in range(at.deep):
                y_copy(j, e, d).wait_recv()
        return jnp.swapaxes(whole[j].reshape(rows, 2, size // 2, wide), 0, 1).reshape(rank, wide)

    def loop(count, body):
        lax.fori_loop(0, count, lambda j, c: (body(j), c)[1], 0)

    work[...] = gram[...]
    x[...] = eye(rank)

    steps = rank // a.shape[0]
    each = blocks // steps

    def step(i):
        factor_step(i, work, x, a, w)

        @pl.when(i > 0)
        def _():
            for k in range(each):
                forward((i - 1) * each + k)

    loop(steps, step)
    xh[...], xl[...] = split(x[...])
    lines = min(256, p.shape[1])
    fetch.wait()

    def left_out(i):
        span = pl.ds(pl.multiple_of(i * lines, lines), lines)
        return [
            pltpu.make_async_copy(left_high.at[span], left_high_far.at[span], left_sem.at[i, 0]),
            pltpu.make_async_copy(left_low.at[span], left_low_far.at[span], left_sem.at[i, 1]),
        ]

    def solved_out(j):
        return pltpu.make_async_copy(solved.at[:, lanes(j)], solved_far.at[:, lanes(j)], solved_sem.at[j])

    def left(i):
        span = pl.ds(pl.multiple_of(i * lines, lines), lines)
        value = three(nn, (xh[...], xl[...]), split(p[:, span])).T
        left_high[span, :], left_low[span, :] = split(value)
        for copy in left_out(i):
            copy.start()

    loop(p.shape[1] // lines, left)
    total[...] = jnp.zeros_like(total)

    def turn(j):
        s = three(nn, (xh[...], xl[...]), split(block(j)))
        sums = total[...]
        for k in range(0, wide, 128):
            sums = sums + s[:, k : k + 128] * s[:, k : k + 128]
        total[...] = sums
        solved[:, lanes(j)] = s
        solved_out(j).start()

        @pl.when((j >= 1) & (j <= each))
        def _():
            forward((steps - 1) * each + j - 1)

    loop(blocks, turn)
    sq[...] = row_sums(total[...])
    go = Sender(ss, sr)
    copies = [go.start(sq, sq_in.at[d], peer) for d, peer in enumerate(col_peers)]
    value = sq[...]
    for d, copy in enumerate(copies):
        copy.wait_recv()
        value = value + sq_in[d]
    norms[...] = jnp.sqrt(value + epsilon)
    go.drain()
    for i in range(p.shape[1] // lines):
        for copy in left_out(i):
            copy.wait()
    for j in range(blocks):
        solved_out(j).wait()
    for j in range(blocks):
        for d in range(1, at.deep):
            z_copy(j, d).wait_send()
        for e in range(1, at.flat):
            for d in range(at.deep):
                y_copy(j, e, d).wait_send()


def gather(rows, cols, ident, own, gram, p):
    size, width = own.shape
    rank, lines = p.shape
    blocks = max(1, min(8, width // 256))
    deep = outer_factor(rows)
    flat = rows // deep
    block = min(128, rank)
    dma = pltpu.SemaphoreType.DMA
    out_shape = [jax.ShapeDtypeStruct((rank, width), f32), jax.ShapeDtypeStruct((8, rank), f32)]
    out_shape += [jax.ShapeDtypeStruct((lines, rank), bf16)] * 2
    scratch = [pltpu.VMEM((blocks, deep, flat, size, width // blocks), f32)]
    scratch += [pltpu.VMEM((rank, rank), f32)] + [pltpu.VMEM((rank, rank), bf16)] * 2
    scratch += [pltpu.VMEM((block, block), f32)] * 2 + [pltpu.VMEM((rank, rank), f32), pltpu.VMEM((rank, 128), f32)]
    scratch += [pltpu.VMEM((8, rank), f32), pltpu.VMEM((cols - 1, 8, rank), f32)] + [dma((cols - 1,))] * 2
    scratch += [pltpu.VMEM((rank, lines), f32), pltpu.VMEM((rank, width), f32)] + [pltpu.VMEM((lines, rank), bf16)] * 2
    scratch += [dma((1,)), dma((blocks,)), dma((lines // min(256, lines), 2))]
    scratch += [dma((blocks, deep - 1))] * 2 + [dma((blocks, flat - 1, deep))] * 2
    return pl.pallas_call(
        functools.partial(gather_kernel, rows, cols, blocks),
        name="gather",
        out_shape=out_shape,
        in_specs=[VMEM, VMEM, FAR],
        out_specs=[FAR, VMEM, FAR, FAR],
        scratch_shapes=scratch,
        compiler_params=pltpu.CompilerParams(collective_id=ident, has_side_effects=True, vmem_limit_bytes=LIMIT),
        cost_estimate=cost(3e10, 16 << 20),
    )(own, gram, p)


def shards(rows, cols, momentum, gradient, weight, right_start):
    out_dim, in_dim = momentum.shape[0] * rows, momentum.shape[1] * cols
    rank = right_start.shape[1] * rows
    high, low, joined, own, gram = iterate(0, rows, cols, 0, right_start.T, momentum, gradient)
    for iteration in range(1, ITERS):
        joined, own, gram = iterate(1, rows, cols, 1, own, gram, high, low)
    own = own.reshape(rank // rows, own.shape[-1])
    products, norms, left_high, left_low = gather(rows, cols, 2, own, gram, joined)
    scale_factor = step_rate * (out_dim * in_dim / rank) ** 0.5
    new_momentum, new_weight, new_right = outputs(
        scale_factor, rank // rows, left_high, left_low, products, norms, momentum, gradient, weight
    )
    return new_momentum, new_weight, new_right.T


def solution(mesh):
    rows, cols = mesh.shape["row"], mesh.shape["col"]
    return jax.shard_map(
        functools.partial(shards, rows, cols),
        mesh=mesh,
        in_specs=(P("row", "col"), P("row", "col"), P("row", "col"), P("col", "row")),
        out_specs=(P("row", "col"), P("row", "col"), P("col", "row")),
        check_vma=False,
    )
```

```python
import functools

import jax
import jax.numpy as jnp
from jax import lax
from jax.experimental import pallas as pl
from jax.experimental.pallas import tpu as pltpu
from jax.sharding import PartitionSpec as P

ITERS = 2
CORES = 2
momentum_decay = 0.9
step_rate = 0.1
epsilon = 1e-06
exact = lax.Precision.HIGHEST
f32, bf16 = jnp.float32, jnp.bfloat16
VMEM = pl.BlockSpec(memory_space=pltpu.VMEM)
FAR = pl.BlockSpec(memory_space=pl.ANY)
MESH = pl.DeviceIdType.MESH
LIMIT = 56 << 20


def nt(a, b, precision=None):
    return lax.dot_general(a, b, (((1,), (1,)), ((), ())), precision=precision, preferred_element_type=f32)


def nn(a, b, precision=None):
    return lax.dot_general(a, b, (((1,), (0,)), ((), ())), precision=precision, preferred_element_type=f32)


def split(x):
    high = x.astype(bf16)
    return high, (x - high.astype(f32)).astype(bf16)


def three(dot, a, b):
    return (dot(a[1], b[0]) + dot(a[0], b[1])) + dot(a[0], b[0])


def outer_factor(n):
    d = 1
    while d * d < n or n % d:
        d += 1
    return d


def cost(flops, moved):
    return pl.CostEstimate(flops=int(flops), bytes_accessed=int(moved), transcendentals=0)


def eye(n):
    return (lax.broadcasted_iota(jnp.int32, (n, n), 0) == lax.broadcasted_iota(jnp.int32, (n, n), 1)).astype(f32)


def eliminate(a, w):
    size = a.shape[0]
    shape = (8, size)
    sub = lax.broadcasted_iota(jnp.int32, shape, 0)
    w[...] = eye(size)
    for at in range(0, size, 8):
        slab, inv_rows = a[at : at + 8, :], w[at : at + 8, :]
        cols = [jnp.broadcast_to(slab[:, at + i : at + i + 1], shape) for i in range(8)]
        scale = jnp.zeros(shape, f32)
        for i in range(8):
            pivot = jnp.broadcast_to(cols[i][i : i + 1, :], shape)
            scale = jnp.where(sub == i, lax.rsqrt(pivot), scale)
            if i < 7:
                m = jnp.where(sub > i, cols[i] / pivot, 0.0)
                for k in range(i + 1, 8):
                    cols[k] = cols[k] - m * jnp.broadcast_to(cols[k][i : i + 1, :], shape)
                slab = slab - m * jnp.broadcast_to(slab[i : i + 1, :], shape)
                inv_rows = inv_rows - m * jnp.broadcast_to(inv_rows[i : i + 1, :], shape)
        upper, inv_rows = slab * scale, inv_rows * scale
        w[at : at + 8, :] = inv_rows
        lower = upper.T
        for k in range(at + 8, size, 8):
            rows, inv = a[k : k + 8, :], w[k : k + 8, :]
            for i in range(8):
                factor = jnp.broadcast_to(lower[k : k + 8, i : i + 1], shape)
                rows = rows - factor * jnp.broadcast_to(upper[i : i + 1, :], shape)
                inv = inv - factor * jnp.broadcast_to(inv_rows[i : i + 1, :], shape)
            a[k : k + 8, :] = rows
            w[k : k + 8, :] = inv


def factor_step(step, work, x, a, w):
    rank, block = work.shape[0], a.shape[0]
    span = pl.ds(pl.multiple_of(step * block, block), block)
    a[...] = work[span, span]
    eliminate(a, w)
    inverse = w[...]
    below = lax.broadcasted_iota(jnp.int32, (rank, block), 0) >= (step + 1) * block
    panel = jnp.where(below, nt(work[:, span], inverse, exact), 0.0)
    solved = nn(inverse, x[span, :], exact)
    x[...] = x[...] - nn(panel, solved, exact)
    x[span, :] = solved
    work[...] = work[...] - nt(panel, panel, exact)


def row_sums(total):
    rank = total.shape[0]
    column = jnp.sum(total, axis=1, keepdims=True)
    return jnp.broadcast_to(column, (rank, 128)).T[:8, :]


def final_kernel(scale_factor, high, low, q, norms, m, g, weight, new_m, new_w, new_r, scaled):
    rank = q.shape[0]
    column = jnp.broadcast_to(norms[0:1, :], (128, rank)).T[:, 0:1]
    s = q[...]
    left = (high[...], low[...])
    blended = m[...] + g[...].astype(f32)
    new_m[...] = blended - (1.0 - momentum_decay) * nn(left[0], s.astype(bf16))
    right = s / column
    scaled[...] = right
    size = new_r.shape[0]
    new_r[...] = scaled[pl.ds(pl.multiple_of(lax.axis_index("row") * size, size), size), :]
    update = three(nn, left, split(right))
    new_w[...] = (weight[...].astype(f32) - scale_factor * update).astype(bf16)


def outputs(scale_factor, size, high, low, q, norms, momentum, gradient, weight):
    rank, cols = q.shape
    rows = high.shape[0]
    wide = min(256, cols)
    side = pl.BlockSpec((rows, rank), lambda j: (0, 0))
    block = pl.BlockSpec((rows, wide), lambda j: (0, j))
    return pl.pallas_call(
        functools.partial(final_kernel, scale_factor),
        name="outputs",
        grid=(cols // wide,),
        in_specs=[side, side, pl.BlockSpec((rank, wide), lambda j: (0, j)), pl.BlockSpec((8, rank), lambda j: (0, 0)), block, block, block],
        out_specs=[block, block, pl.BlockSpec((size, wide), lambda j: (0, j))],
        out_shape=[
            jax.ShapeDtypeStruct((rows, cols), f32),
            jax.ShapeDtypeStruct((rows, cols), bf16),
            jax.ShapeDtypeStruct((size, cols), f32),
        ],
        scratch_shapes=[pltpu.VMEM((rank, wide), f32)],
        compiler_params=pltpu.CompilerParams(vmem_limit_bytes=LIMIT),
        cost_estimate=cost(8 * rank * rows * cols, 14 * rows * cols),
    )(high, low, q, norms, momentum, gradient, weight)


class Place:
    def __init__(self, rows, cols):
        self.deep = outer_factor(rows)
        self.flat = rows // self.deep
        self.wide = cols // CORES
        self.row, self.col = lax.axis_index("row"), lax.axis_index("col")
        self.z, self.y = self.row // self.flat, self.row % self.flat
        self.x, self.core = self.col // CORES, self.col % CORES

    def to_y(self, d):
        return (self.z * self.flat + (self.y + d) % self.flat, self.col)

    def to_z(self, d):
        return (((self.z + d) % self.deep) * self.flat + self.y, self.col)

    def to_x(self, d):
        return (self.row, ((self.x + d) % self.wide) * CORES + self.core)

    def partner(self):
        return (self.row, self.x * CORES + 1 - self.core)

    def y_peers(self):
        return [self.to_y(d) for d in range(1, self.flat)]

    def z_peers(self):
        return [self.to_z(d) for d in range(1, self.deep)]

    def x_peers(self):
        return [self.to_x(d) for d in range(1, self.wide)]


def greet(peers):
    barrier = pltpu.get_barrier_semaphore()
    for peer in peers:
        pl.semaphore_signal(barrier, inc=1, device_id=peer, device_id_type=MESH)
    pl.semaphore_wait(barrier, len(peers))


class Sender:
    def __init__(self, send, recv):
        self.send, self.recv, self.copies = send, recv, []

    def start(self, src, dst, peer):
        at = len(self.copies)
        copy = pltpu.make_async_remote_copy(
            src_ref=src, dst_ref=dst, send_sem=self.send.at[at], recv_sem=self.recv.at[at], device_id=peer, device_id_type=MESH
        )
        copy.start()
        self.copies.append(copy)
        return copy

    def drain(self):
        for copy in self.copies:
            copy.wait_send()


PIECES = 4


def iterate_kernel(rows, cols, units, blocks, mode, *refs):
    if mode == 0:
        own, m_far, g_far, high_far, low_far, chunk, gall = refs[:7]
        out, m, g, high, low, in_sem, out_sem = refs[7:14]
        refs = refs[14:]
    else:
        own, gram, high_far, low_far, out, chunk, gall = refs[:7]
        x, xh, xl, a, w, work, total, sq, sq_in, ss, sr, high, low, in_sem = refs[7:21]
        refs = refs[21:]
    whole, part, half, near, far, gram_own, ph, pw, q, qy, h, hz, gq, gyr, gh, gzr, zs, zr, ys, yr = refs[:20]
    join_s, join_r, far_s, far_r, back_s, back_r, qy_s, qy_r, hz_s, hz_r, send, recv = refs[20:]
    at = Place(rows, cols)
    peers = at.y_peers() + at.z_peers()
    col_peers = [(at.row, (at.col + d) % cols) for d in range(1, cols)]
    greet(peers + (col_peers if mode else at.x_peers() + [at.partner()]))
    size, wide = whole.shape[3], whole.shape[4]
    rank, middle_rank = size * rows * (2 if mode else 1), part.shape[1] * part.shape[2] * part.shape[3]
    lines = part.shape[-1]
    step_lanes = units // 2

    def remote(src, dst, send_sem, recv_sem, peer):
        return pltpu.make_async_remote_copy(
            src_ref=src, dst_ref=dst, send_sem=send_sem, recv_sem=recv_sem, device_id=peer, device_id_type=MESH
        )

    def spread(at_index, count):
        if isinstance(at_index, int):
            return slice(at_index * count, (at_index + 1) * count)
        return pl.ds(pl.multiple_of(at_index * count, count), count)

    def loop(start, count, body):
        lax.fori_loop(start, count, lambda j, c: (body(j), c)[1], 0)

    split_lines = high.shape[0] // units

    def fetch(j):
        span = spread(j, split_lines)
        pairs = ((m_far, m), (g_far, g)) if mode == 0 else ((high_far, high), (low_far, low))
        return [pltpu.make_async_copy(src.at[span], dst.at[span], in_sem.at[j, i]) for i, (src, dst) in enumerate(pairs)]

    def keep(j):
        span = spread(j, split_lines)
        pairs = ((high, high_far), (low, low_far))
        return [pltpu.make_async_copy(src.at[span], dst.at[span], out_sem.at[j, i]) for i, (src, dst) in enumerate(pairs)]

    def lanes(u):
        return spread(u % step_lanes, wide) if mode else spread(u, wide)

    def source(u):
        return own.at[u // step_lanes, :, lanes(u)] if mode else own.at[:, lanes(u)]

    def z_copy(u, d):
        return remote(source(u), whole.at[u, at.z, at.y], zs.at[u, d - 1], zr.at[u, d - 1], at.to_z(d))

    def y_copy(u, e, d):
        piece = whole.at[u, (at.z - d + at.deep) % at.deep, at.y]
        return remote(source(u) if d == 0 else piece, piece, ys.at[u, e - 1, d], yr.at[u, e - 1, d], at.to_y(e))

    for u in range(units):
        for d in range(1, at.deep):
            z_copy(u, d).start()
        for e in range(1, at.flat):
            y_copy(u, e, 0).start()
    for u in range(units):
        for copy in fetch(u):
            copy.start()
    for u in range(units):
        whole[u, at.z, at.y] = own[u // step_lanes, :, lanes(u)] if mode else own[:, lanes(u)]

    def forward(u):
        for d in range(1, at.deep):
            z_copy(u, d).wait_recv()
            for e in range(1, at.flat):
                y_copy(u, e, d).start()

    def arrived(u):
        for e in range(1, at.flat):
            for d in range(at.deep):
                y_copy(u, e, d).wait_recv()

    mine, other = at.core, 1 - at.core

    def near_copy(r, k):
        return remote(part.at[r, other, k], near.at[r, k], join_s.at[r, k], join_r.at[r, k], at.partner())

    def far_copy(r, k, d):
        return remote(half.at[r, k], far.at[r, d - 1, k], far_s.at[r, k, d - 1], far_r.at[r, k, d - 1], at.to_x(d))

    def back_copy(r, k):
        return remote(out.at[r, mine, k], out.at[r, mine, k], back_s.at[r, k], back_r.at[r, k], at.partner())

    def sq_copy(r, d):
        return remote(sq.at[r], sq_in.at[r, d - 1], ss.at[r, d - 1], sr.at[r, d - 1], (at.row, (at.col + d) % cols))

    def join_begin(r):
        if mode:
            sq[r] = row_sums(total[r])
            for d in range(1, cols):
                sq_copy(r, d).start()
        for k in range(PIECES):
            near_copy(r, k).start()
        for k in range(PIECES):
            near_copy(r, k).wait_recv()
            half[r, k] = part[r, mine, k] + near[r, k]
            for d in range(1, at.wide):
                far_copy(r, k, d).start()

    def join_end(r):
        if mode:
            value = sq[r]
            for d in range(1, cols):
                sq_copy(r, d).wait_recv()
                value = value + sq_in[r, d - 1]
            norm = jnp.sqrt(value + epsilon)
            column = jnp.broadcast_to(norm[0:1, :], (128, middle_rank)).T[:, 0:1]
            count = middle_rank // (CORES * PIECES)
        for k in range(PIECES):
            value = half[r, k]
            for d in range(1, at.wide):
                far_copy(r, k, d).wait_recv()
                value = value + far[r, d - 1, k]
            if mode:
                first = column[k * count : (k + 1) * count]
                value = value / jnp.where(mine == 0, first, column[(PIECES + k) * count : (PIECES + k + 1) * count])
            out[r, mine, k] = value
            back_copy(r, k).start()
        for k in range(PIECES):
            back_copy(r, k).wait_recv()

    q_size, q_wide = q.shape[4], q.shape[5]

    def qy_copy(r, j, e):
        return remote(q.at[r, j, :, (at.y + e) % at.flat], qy.at[r, j, e - 1], qy_s.at[r, j, e - 1], qy_r.at[r, j, e - 1], at.to_y(e))

    def hz_copy(r, j, d):
        return remote(h.at[r, j, (at.z + d) % at.deep], hz.at[r, j, d - 1], hz_s.at[r, j, d - 1], hz_r.at[r, j, d - 1], at.to_z(d))

    def multiply(r):
        ph[...], pw[...] = split(out[r].reshape(middle_rank, lines))

        def turn(j):
            columns = spread(j, q_wide)
            value = three(nn, (ph[...], pw[...]), (high[:, columns], low[:, columns]))
            q[r, j] = value.reshape(at.deep, at.flat, q_size, q_wide)
            for e in range(1, at.flat):
                qy_copy(r, j, e).start()

        loop(0, blocks, turn)

    def middle(r, j):
        value = q[r, j, :, pl.ds(at.y, 1)][:, 0]
        for e in range(1, at.flat):
            qy_copy(r, j, e).wait_recv()
            value = value + qy[r, j, e - 1]
        h[r, j] = value
        for d in range(1, at.deep):
            hz_copy(r, j, d).start()

    def last(r, j):
        value = h[r, j, pl.ds(at.z, 1)][0]
        for d in range(1, at.deep):
            hz_copy(r, j, d).wait_recv()
            value = value + hz[r, j, d - 1]
        chunk[r, :, spread(j, q_wide)] = value

    def add(r, u, value):
        product = three(nt, split(value), (high[:, lanes(u)], low[:, lanes(u)]))

        @pl.when(lanes_at(u) == 0)
        def _():
            if mode:
                part[r] = product.reshape(part.shape[1:])
            else:
                part[...] = product.reshape(part.shape)

        @pl.when(lanes_at(u) > 0)
        def _():
            if mode:
                part[r] = part[r] + product.reshape(part.shape[1:])
            else:
                part[...] = part[...] + product.reshape(part.shape)

    def lanes_at(u):
        return u % step_lanes if mode else u

    if mode == 0:
        def divide(j):
            span = spread(j, split_lines)
            for copy in fetch(j):
                copy.wait()
            high[span, :], low[span, :] = split(m[span, :] + g[span, :].astype(f32))
            for copy in keep(j):
                copy.start()

        loop(0, units, divide)
        forward(0)

        def turn(u):
            forward(u + 1)
            arrived(u)
            add(0, u, whole[u].reshape(rank, wide))

        loop(0, units - 1, turn)
        arrived(units - 1)
        add(0, jnp.int32(units - 1), whole[units - 1].reshape(rank, wide))
        join_begin(0)
        join_begin(1)
    else:
        work[...] = gram[...]
        x[...] = eye(rank)

        def step(u):
            factor_step(u, work, x, a, w)

            @pl.when(u > 0)
            def _():
                forward(u - 1)

        loop(0, units, step)
        xh[...], xl[...] = split(x[...])
        total[...] = jnp.zeros_like(total)
        for u in range(units):
            for copy in fetch(u):
                copy.wait()

        def solve(r, u):
            arrived(u)
            span = slice(r * middle_rank, (r + 1) * middle_rank)
            s = jnp.zeros((middle_rank, wide), f32)
            for k in range(r + 1):
                columns = slice(k * middle_rank, (k + 1) * middle_rank)
                value = whole[u - (r - k) * step_lanes].reshape(middle_rank, wide)
                s = s + three(nn, (xh[span, columns], xl[span, columns]), split(value))
            sums = total[r]
            for k in range(0, wide, 128):
                sums = sums + s[:, k : k + 128] * s[:, k : k + 128]
            total[r] = sums
            add(r, u, s)

        loop(0, step_lanes, lambda u: solve(0, u))
        join_begin(0)
        forward(units - 1)
        loop(step_lanes, units, lambda u: solve(1, u))
        join_begin(1)

    join_end(0)
    multiply(0)
    middle(0, 0)
    join_end(1)
    own_rows = gram_own.shape[0]
    shares = PIECES * part.shape[3] // own_rows
    place = at.col // shares
    take = own_rows // part.shape[3]
    picked = out[place // CORES, place % CORES, pl.ds((at.col % shares) * take, take)].reshape(own_rows, lines)
    gram_own[...] = nt(picked, out[...].reshape(2 * middle_rank, lines), exact)
    share = gq.shape[2]
    for i in range(at.deep):
        for j in range(at.flat):
            k = (i * at.flat + j) * share
            gq[i, j] = gram_own[k : k + share, :]
    go = Sender(send, recv)
    gy = [go.start(gq.at[:, (at.y + e) % at.flat], gyr.at[e - 1], at.to_y(e)) for e in range(1, at.flat)]
    multiply(1)
    loop(1, blocks, lambda j: middle(0, j))
    value = gq[:, pl.ds(at.y, 1)][:, 0]
    for d, copy in enumerate(gy):
        copy.wait_recv()
        value = value + gyr[d]
    gh[...] = value
    gz = [go.start(gh.at[(at.z + d) % at.deep], gzr.at[d - 1], at.to_z(d)) for d in range(1, at.deep)]
    loop(0, blocks, lambda j: last(0, j))
    middle(1, 0)
    value = gh[pl.ds(at.z, 1)][0]
    for d, copy in enumerate(gz):
        copy.wait_recv()
        value = value + gzr[d]
    here = (at.x, at.core, at.z, at.y)
    gall[here] = value
    gz = [go.start(gall.at[here], gall.at[here], peer) for peer in at.z_peers()]
    loop(1, (blocks + 1) // 2, lambda j: middle(1, j))
    for copy in gz:
        copy.wait_recv()
    line_at = (at.x, at.core, slice(None), at.y)
    gy = [go.start(gall.at[line_at], gall.at[line_at], peer) for peer in at.y_peers()]
    loop((blocks + 1) // 2, blocks, lambda j: middle(1, j))
    for copy in gy:
        copy.wait_recv()
    gx = [go.start(gall.at[at.x, at.core], gall.at[at.x, at.core], peer) for peer in at.x_peers()]
    loop(0, blocks - 1, lambda j: last(1, j))
    for copy in gx:
        copy.wait_recv()
    gc = go.start(gall.at[:, at.core], gall.at[:, at.core], at.partner())
    last(1, blocks - 1)
    gc.wait_recv()
    go.drain()

    def finish(u):
        if mode == 0:
            for copy in keep(u):
                copy.wait()
        for d in range(1, at.deep):
            z_copy(u, d).wait_send()
        for e in range(1, at.flat):
            for d in range(at.deep):
                y_copy(u, e, d).wait_send()

    loop(0, units, finish)
    for r in range(2):
        for k in range(PIECES):
            near_copy(r, k).wait_send()
            back_copy(r, k).wait_send()
            for d in range(1, at.wide):
                far_copy(r, k, d).wait_send()
        if mode:
            for d in range(1, cols):
                sq_copy(r, d).wait_send()

        def sent(j):
            for e in range(1, at.flat):
                qy_copy(r, j, e).wait_send()
            for d in range(1, at.deep):
                hz_copy(r, j, d).wait_send()

        loop(0, blocks, sent)


def iterate(mode, rows, cols, ident, own, *args):
    width = own.shape[-1]
    lines = args[-1].shape[0]
    rank = own.size // width * rows
    deep = outer_factor(rows)
    flat = rows // deep
    xs = cols // CORES
    units = 4
    size = rank // rows // (2 if mode else 1)
    wide = width // units * (2 if mode else 1)
    blocks = max(1, min(4, width // 256))
    half_rank, q_wide, q_size = rank // 2, width // blocks, rank // rows // 2
    piece = half_rank // (CORES * PIECES)
    share = rank // cols // rows
    dma = pltpu.SemaphoreType.DMA
    out_shape = [
        jax.ShapeDtypeStruct((2, CORES, PIECES, piece, lines), f32),
        jax.ShapeDtypeStruct((2, q_size, width), f32),
        jax.ShapeDtypeStruct((xs, CORES, deep, flat, share, rank), f32),
    ]
    scratch = []
    if mode == 0:
        out_shape = [jax.ShapeDtypeStruct((lines, width), bf16)] * 2 + out_shape[1:]
        scratch = [pltpu.VMEM((2, CORES, PIECES, piece, lines), f32)]
        scratch += [pltpu.VMEM((lines, width), dtype) for dtype in (f32, bf16, bf16, bf16)] + [dma((units, 2))] * 2
    else:
        block = rank // units
        scratch = [pltpu.VMEM((rank, rank), f32)] + [pltpu.VMEM((rank, rank), bf16)] * 2
        scratch += [pltpu.VMEM((block, block), f32)] * 2 + [pltpu.VMEM((rank, rank), f32), pltpu.VMEM((2, half_rank, 128), f32)]
        scratch += [pltpu.VMEM((2, 8, half_rank), f32), pltpu.VMEM((2, cols - 1, 8, half_rank), f32)]
        scratch += [dma((2, cols - 1))] * 2
        scratch += [pltpu.VMEM((lines, width), bf16)] * 2 + [dma((units, 2))]
    scratch += [
        pltpu.VMEM((units, deep, flat, size, wide), f32),
        pltpu.VMEM((2, CORES, PIECES, piece, lines), f32),
        pltpu.VMEM((2, PIECES, piece, lines), f32),
        pltpu.VMEM((2, PIECES, piece, lines), f32),
        pltpu.VMEM((2, xs - 1, PIECES, piece, lines), f32),
        pltpu.VMEM((rank // cols, rank), f32),
        pltpu.VMEM((half_rank, lines), bf16),
        pltpu.VMEM((half_rank, lines), bf16),
        pltpu.VMEM((2, blocks, deep, flat, q_size, q_wide), f32),
        pltpu.VMEM((2, blocks, flat - 1, deep, q_size, q_wide), f32),
        pltpu.VMEM((2, blocks, deep, q_size, q_wide), f32),
        pltpu.VMEM((2, blocks, deep - 1, q_size, q_wide), f32),
        pltpu.VMEM((deep, flat, share, rank), f32),
        pltpu.VMEM((flat - 1, deep, share, rank), f32),
        pltpu.VMEM((deep, share, rank), f32),
        pltpu.VMEM((deep - 1, share, rank), f32),
    ]
    scratch += [dma((units, deep - 1))] * 2 + [dma((units, flat - 1, deep))] * 2
    scratch += [dma((2, PIECES))] * 2 + [dma((2, PIECES, xs - 1))] * 2 + [dma((2, PIECES))] * 2
    scratch += [dma((2, blocks, flat - 1))] * 2 + [dma((2, blocks, deep - 1))] * 2
    scratch += [dma((2 * (deep - 1) + 2 * (flat - 1) + xs,))] * 2
    res = pl.pallas_call(
        functools.partial(iterate_kernel, rows, cols, units, blocks, mode),
        name="iterate",
        out_shape=out_shape,
        in_specs=[VMEM] * (len(args) - 1) + [FAR] * 2,
        out_specs=[VMEM] * 3 if mode else [FAR] * 2 + [VMEM] * 2,
        scratch_shapes=scratch,
        compiler_params=pltpu.CompilerParams(collective_id=ident, has_side_effects=True, vmem_limit_bytes=LIMIT),
        cost_estimate=cost(6e10, 24 << 20),
    )(own, *args)
    first = [res[0].reshape(rank, lines)] if mode else list(res[:2])
    return first + [res[-2], res[-1].reshape(rank, rank)]


def gather_kernel(rows, cols, blocks, *refs):
    own, gram, p_far, solved_far, norms, left_high_far, left_low_far = refs[:7]
    whole, x, xh, xl, a, w, work, total, sq, sq_in, ss, sr = refs[7:19]
    p, solved, left_high, left_low, p_sem, solved_sem, left_sem, zs, zr, ys, yr = refs[19:]
    at = Place(rows, cols)
    col_peers = [(at.row, (at.col + d) % cols) for d in range(1, cols)]
    greet(at.y_peers() + at.z_peers() + col_peers)
    wide, size = whole.shape[-1], own.shape[0]
    rank = size * rows

    def lanes(j):
        if isinstance(j, int):
            return slice(j * wide, (j + 1) * wide)
        return pl.ds(pl.multiple_of(j * wide, wide), wide)

    def z_copy(j, d):
        return pltpu.make_async_remote_copy(
            src_ref=own.at[:, lanes(j)],
            dst_ref=whole.at[j, at.z, at.y],
            send_sem=zs.at[j, d - 1],
            recv_sem=zr.at[j, d - 1],
            device_id=at.to_z(d),
            device_id_type=MESH,
        )

    def y_copy(j, e, d):
        chunk = whole.at[j, (at.z - d + at.deep) % at.deep, at.y]
        return pltpu.make_async_remote_copy(
            src_ref=own.at[:, lanes(j)] if d == 0 else chunk,
            dst_ref=chunk,
            send_sem=ys.at[j, e - 1, d],
            recv_sem=yr.at[j, e - 1, d],
            device_id=at.to_y(e),
            device_id_type=MESH,
        )

    for j in range(blocks):
        for d in range(1, at.deep):
            z_copy(j, d).start()
        for e in range(1, at.flat):
            y_copy(j, e, 0).start()
    fetch = pltpu.make_async_copy(p_far, p, p_sem.at[0])
    fetch.start()
    for j in range(blocks):
        whole[j, at.z, at.y] = own[:, lanes(j)]

    def forward(j):
        for d in range(1, at.deep):
            z_copy(j, d).wait_recv()
            for e in range(1, at.flat):
                y_copy(j, e, d).start()

    def block(j):
        for e in range(1, at.flat):
            for d in range(at.deep):
                y_copy(j, e, d).wait_recv()
        return jnp.swapaxes(whole[j].reshape(rows, 2, size // 2, wide), 0, 1).reshape(rank, wide)

    def loop(count, body):
        lax.fori_loop(0, count, lambda j, c: (body(j), c)[1], 0)

    work[...] = gram[...]
    x[...] = eye(rank)

    steps = rank // a.shape[0]
    each = blocks // steps

    def step(i):
        factor_step(i, work, x, a, w)

        @pl.when(i > 0)
        def _():
            for k in range(each):
                forward((i - 1) * each + k)

    loop(steps, step)
    xh[...], xl[...] = split(x[...])
    lines = min(256, p.shape[1])
    fetch.wait()

    def left_out(i):
        span = pl.ds(pl.multiple_of(i * lines, lines), lines)
        return [
            pltpu.make_async_copy(left_high.at[span], left_high_far.at[span], left_sem.at[i, 0]),
            pltpu.make_async_copy(left_low.at[span], left_low_far.at[span], left_sem.at[i, 1]),
        ]

    def solved_out(j):
        return pltpu.make_async_copy(solved.at[:, lanes(j)], solved_far.at[:, lanes(j)], solved_sem.at[j])

    def left(i):
        span = pl.ds(pl.multiple_of(i * lines, lines), lines)
        value = three(nn, (xh[...], xl[...]), split(p[:, span])).T
        left_high[span, :], left_low[span, :] = split(value)
        for copy in left_out(i):
            copy.start()

    loop(p.shape[1] // lines, left)
    total[...] = jnp.zeros_like(total)

    def turn(j):
        s = three(nn, (xh[...], xl[...]), split(block(j)))
        sums = total[...]
        for k in range(0, wide, 128):
            sums = sums + s[:, k : k + 128] * s[:, k : k + 128]
        total[...] = sums
        solved[:, lanes(j)] = s
        solved_out(j).start()

        @pl.when((j >= 1) & (j <= each))
        def _():
            forward((steps - 1) * each + j - 1)

    loop(blocks, turn)
    sq[...] = row_sums(total[...])
    go = Sender(ss, sr)
    copies = [go.start(sq, sq_in.at[d], peer) for d, peer in enumerate(col_peers)]
    value = sq[...]
    for d, copy in enumerate(copies):
        copy.wait_recv()
        value = value + sq_in[d]
    norms[...] = jnp.sqrt(value + epsilon)
    go.drain()
    for i in range(p.shape[1] // lines):
        for copy in left_out(i):
            copy.wait()
    for j in range(blocks):
        solved_out(j).wait()
    for j in range(blocks):
        for d in range(1, at.deep):
            z_copy(j, d).wait_send()
        for e in range(1, at.flat):
            for d in range(at.deep):
                y_copy(j, e, d).wait_send()


def gather(rows, cols, ident, own, gram, p):
    size, width = own.shape
    rank, lines = p.shape
    blocks = max(1, min(8, width // 256))
    deep = outer_factor(rows)
    flat = rows // deep
    block = min(128, rank)
    dma = pltpu.SemaphoreType.DMA
    out_shape = [jax.ShapeDtypeStruct((rank, width), f32), jax.ShapeDtypeStruct((8, rank), f32)]
    out_shape += [jax.ShapeDtypeStruct((lines, rank), bf16)] * 2
    scratch = [pltpu.VMEM((blocks, deep, flat, size, width // blocks), f32)]
    scratch += [pltpu.VMEM((rank, rank), f32)] + [pltpu.VMEM((rank, rank), bf16)] * 2
    scratch += [pltpu.VMEM((block, block), f32)] * 2 + [pltpu.VMEM((rank, rank), f32), pltpu.VMEM((rank, 128), f32)]
    scratch += [pltpu.VMEM((8, rank), f32), pltpu.VMEM((cols - 1, 8, rank), f32)] + [dma((cols - 1,))] * 2
    scratch += [pltpu.VMEM((rank, lines), f32), pltpu.VMEM((rank, width), f32)] + [pltpu.VMEM((lines, rank), bf16)] * 2
    scratch += [dma((1,)), dma((blocks,)), dma((lines // min(256, lines), 2))]
    scratch += [dma((blocks, deep - 1))] * 2 + [dma((blocks, flat - 1, deep))] * 2
    return pl.pallas_call(
        functools.partial(gather_kernel, rows, cols, blocks),
        name="gather",
        out_shape=out_shape,
        in_specs=[VMEM, VMEM, FAR],
        out_specs=[FAR, VMEM, FAR, FAR],
        scratch_shapes=scratch,
        compiler_params=pltpu.CompilerParams(collective_id=ident, has_side_effects=True, vmem_limit_bytes=LIMIT),
        cost_estimate=cost(3e10, 16 << 20),
    )(own, gram, p)


def shards(rows, cols, momentum, gradient, weight, right_start):
    out_dim, in_dim = momentum.shape[0] * rows, momentum.shape[1] * cols
    rank = right_start.shape[1] * rows
    high, low, own, gram = iterate(0, rows, cols, 0, right_start.T, momentum, gradient)
    for iteration in range(1, ITERS):
        joined, own, gram = iterate(1, rows, cols, 1, own, gram, high, low)
    own = own.reshape(rank // rows, own.shape[-1])
    products, norms, left_high, left_low = gather(rows, cols, 2, own, gram, joined)
    scale_factor = step_rate * (out_dim * in_dim / rank) ** 0.5
    new_momentum, new_weight, new_right = outputs(
        scale_factor, rank // rows, left_high, left_low, products, norms, momentum, gradient, weight
    )
    return new_momentum, new_weight, new_right.T


def solution(mesh):
    rows, cols = mesh.shape["row"], mesh.shape["col"]
    return jax.shard_map(
        functools.partial(shards, rows, cols),
        mesh=mesh,
        in_specs=(P("row", "col"), P("row", "col"), P("row", "col"), P("col", "row")),
        out_specs=(P("row", "col"), P("row", "col"), P("col", "row")),
        check_vma=False,
    )
```
